512 devices in a mesh: row: 16 (over x, z_hi), col: 32 (over z_lo, y, core).
Axes of the slice: x: 4, y: 8, z: 8 (z_hi: 4, z_lo: 2; z = z_hi * 2 + z_lo), core: 2. Of those that a mesh axis runs over, the one named last changes fastest.
Arguments:
- bin_features: bfloat16 [4096, 512], P('row'), may hold values from -6 to 6
- w_left: bfloat16 [512, 32], replicated, may hold values from -0.25 to 0.25
- w_right: bfloat16 [512, 32], replicated, may hold values from -0.25 to 0.25
- depth_kernel: float32 [9, 32], replicated, may hold values from -2 to 2
- w_point: bfloat16 [32, 32], replicated, may hold values from -1 to 1
- w_head: bfloat16 [32, 24], replicated, may hold values from -1 to 1
- cotangent: bfloat16 [24, 4096, 4096], P(None, 'row', 'col'), may hold values from -6 to 6
Outputs:
- grad_features: bfloat16 [4096, 512], P('row')
- grad_w_left: float32 [512, 32], replicated
- grad_w_right: float32 [512, 32], replicated
- grad_kernel: float32 [9, 32], replicated
- grad_point: float32 [32, 32], replicated
- grad_head: float32 [32, 24], replicated
The draws below stay inside these ranges and needn't reach their ends.
All inputs are finite; a program needn't handle non-finite values.
Results may differ from the reference program's by a relative error of at most 0.019.
Values may be sent and summed in bfloat16 or wider, within the bound.
No kernel may reach another device: no remote copies, remote signals or barrier semaphores. Data moves between devices by JAX's collectives and lax.ppermute only.
A program may use at most 64 MiB of HBM per device.

```python
import math
import jax
import jax.numpy as jnp
from jax import lax

D = 512
CH = 32
HEADS = 24
DILATION_STEP = 4
NB = 4096


def level_of(rng, dims, cuts, least, top_value):
    def one(dim, shards_of):
        heights = jax.random.uniform(jax.random.fold_in(jax.random.fold_in(rng, 6), dim), (shards_of,), jnp.float32, least / len(cuts), top_value / len(cuts))
        return jnp.repeat(jnp.exp(heights), dims[dim] // shards_of).reshape((-1,) + (1,) * (len(dims) - dim - 1))

    gain = one(*cuts[0])
    for cut in cuts[1:]:
        gain = gain * one(*cut)
    return gain


def centred(rng, shape, spread, limit, split=(), held_as=jnp.bfloat16):
    loudness = level_of(rng, shape, split, -0.22, 0.18) if split else 1.0
    result = jax.random.normal(rng, shape, jnp.float32) * spread * loudness
    return jnp.minimum(jnp.maximum(result, -limit), limit).astype(held_as)


def setup_inputs(seed: int = 0) -> dict:
    arg_keys = jax.random.split(jax.random.key(seed), 8)
    return {
        "bin_features": centred(arg_keys[0], (NB, D), 1.0, 6.0, ((0, 16),)),
        "w_left": centred(arg_keys[1], (D, CH), D ** -0.5, 0.25),
        "w_right": centred(arg_keys[2], (D, CH), D ** -0.5, 0.25),
        "depth_kernel": centred(arg_keys[3], (9, CH), 9 ** -0.5, 2.0, (), jnp.float32),
        "w_point": centred(arg_keys[4], (CH, CH), CH ** -0.5, 1.0),
        "w_head": centred(arg_keys[5], (CH, HEADS), CH ** -0.5, 1.0),
        "cotangent": centred(arg_keys[6], (HEADS, NB, NB), 1.0, 6.0, ((1, 16), (2, 32))),
    }


def silu_slope(values):
    logistic = jax.nn.sigmoid(values)
    return logistic * (1.0 + values * (1.0 - logistic))

def rounded(values):
    return lax.optimization_barrier(values.astype(jnp.bfloat16)).astype(jnp.float32)

def reference(bin_features, w_left, w_right, depth_kernel, w_point, w_head, cotangent):
    contact_map_bins = bin_features.shape[0]
    chans = w_left.shape[1]
    head_count = w_head.shape[1]
    grad_scale = 1.0 / math.sqrt(contact_map_bins)
    left_proj = jnp.dot(bin_features, w_left, preferred_element_type=jnp.float32).astype(jnp.bfloat16)
    right_projection = jnp.dot(bin_features, w_right, preferred_element_type=jnp.float32).astype(jnp.bfloat16)
    rows_per_block = math.gcd(contact_map_bins, 128)
    block_count = contact_map_bins // rows_per_block
    border_margin = 2 * DILATION_STEP
    extended_rows = rows_per_block + 2 * DILATION_STEP
    left_pad = jnp.pad(left_proj.astype(jnp.float32), ((border_margin, border_margin), (0, 0))).T
    right_padding = jnp.pad(right_projection.astype(jnp.float32), ((DILATION_STEP, DILATION_STEP), (0, 0))).T
    row_place = jnp.arange(contact_map_bins + 2 * border_margin) - border_margin
    row_valid = jnp.where((row_place >= 0) & (row_place < contact_map_bins), 1.0, 0.0).astype(jnp.float32)
    column_position = jnp.arange(contact_map_bins + 2 * DILATION_STEP) - DILATION_STEP
    col_valid = jnp.where((column_position >= 0) & (column_position < contact_map_bins), 1.0, 0.0).astype(jnp.float32)
    head_padding = jnp.pad(cotangent, ((0, 0), (DILATION_STEP, DILATION_STEP), (0, 0)))
    kernel_taps = depth_kernel.astype(jnp.float32)
    point_weight = w_point.astype(jnp.float32)
    head_weight = w_head.astype(jnp.float32)

    def one_block(totals, row_start):
        kern_acc, pointwise_running_sum, head_running_sum, right_acc = totals
        row_slab = lax.dynamic_slice_in_dim(left_pad, row_start, rows_per_block + 2 * border_margin, 1)
        slab_valid = lax.dynamic_slice_in_dim(row_valid, row_start, rows_per_block + 2 * border_margin, 0)
        extended_pair = rounded((row_slab[:, :, None] + right_padding[:, None, :]) * (slab_valid[:, None] * col_valid[None, :])[None])
        convolved_map = jnp.zeros((chans, extended_rows, contact_map_bins), jnp.float32)
        for kernel_tap_row in range(3):
            for kernel_tap_column in range(3):
                convolved_map = convolved_map + kernel_taps[3 * kernel_tap_row + kernel_tap_column][:, None, None] * extended_pair[:, DILATION_STEP * kernel_tap_row:DILATION_STEP * kernel_tap_row + extended_rows, DILATION_STEP * kernel_tap_column:DILATION_STEP * kernel_tap_column + contact_map_bins]
        hidden_state = rounded(jax.nn.silu(convolved_map))
        mixed_out = jnp.einsum('co,cij->oij', point_weight, hidden_state)
        centre_offset = extended_pair[:, DILATION_STEP:DILATION_STEP + extended_rows, DILATION_STEP:DILATION_STEP + contact_map_bins]
        trunk_matrix = rounded(centre_offset + mixed_out)
        head_weight_block = lax.dynamic_slice_in_dim(head_padding, row_start, extended_rows, 1).astype(jnp.float32)
        trunk_gradient = rounded(grad_scale * jnp.einsum('ch,hij->cij', head_weight, head_weight_block))
        grad_hidden = jnp.einsum('co,oij->cij', point_weight, trunk_gradient)
        convolved_gradient = rounded(grad_hidden * silu_slope(convolved_map))
        padded_convolved_gradient = jnp.pad(convolved_gradient, ((0, 0), (0, 0), (DILATION_STEP, DILATION_STEP)))
        inner_convolved = convolved_gradient[:, DILATION_STEP:DILATION_STEP + rows_per_block]
        backward_pass = jnp.zeros((chans, rows_per_block, contact_map_bins), jnp.float32)
        kern_terms = []
        for kernel_tap_row in range(3):
            for kernel_tap_column in range(3):
                backward_pass = backward_pass + kernel_taps[3 * kernel_tap_row + kernel_tap_column][:, None, None] * padded_convolved_gradient[:, DILATION_STEP * (2 - kernel_tap_row):DILATION_STEP * (2 - kernel_tap_row) + rows_per_block, DILATION_STEP * (2 - kernel_tap_column):DILATION_STEP * (2 - kernel_tap_column) + contact_map_bins]
                shifted_window = extended_pair[:, DILATION_STEP + DILATION_STEP * kernel_tap_row:DILATION_STEP + DILATION_STEP * kernel_tap_row + rows_per_block, DILATION_STEP * kernel_tap_column:DILATION_STEP * kernel_tap_column + contact_map_bins]
                kern_terms.append(lax.optimization_barrier(jnp.sum(inner_convolved * shifted_window, axis=(1, 2))))
        pair_gradient = trunk_gradient[:, DILATION_STEP:DILATION_STEP + rows_per_block] + backward_pass
        left_out = lax.optimization_barrier(jnp.sum(pair_gradient, axis=2)).T
        right_acc = right_acc + lax.optimization_barrier(jnp.sum(pair_gradient, axis=1))
        pointwise_running_sum = pointwise_running_sum + jnp.einsum('fsk,gsk->fg', hidden_state[:, DILATION_STEP:DILATION_STEP + rows_per_block], trunk_gradient[:, DILATION_STEP:DILATION_STEP + rows_per_block])
        head_running_sum = head_running_sum + jnp.einsum('ydq,gdq->yg', trunk_matrix[:, DILATION_STEP:DILATION_STEP + rows_per_block], head_weight_block[:, DILATION_STEP:DILATION_STEP + rows_per_block])
        kern_acc = kern_acc + jnp.stack(kern_terms)
        return ((kern_acc, pointwise_running_sum, head_running_sum, right_acc), left_out)
    starts = (jnp.arange(block_count) * rows_per_block).astype(jnp.int32)
    initial = (jnp.zeros((9, chans), jnp.float32), jnp.zeros((chans, chans), jnp.float32), jnp.zeros((chans, head_count), jnp.float32), jnp.zeros((chans, contact_map_bins), jnp.float32))
    totals, left_blocks = lax.scan(one_block, initial, starts)
    kern_acc, pointwise_running_sum, head_running_sum, right_acc = totals
    grad_left = left_blocks.reshape(contact_map_bins, chans).astype(jnp.bfloat16)
    grad_right = right_acc.T.astype(jnp.bfloat16)
    grad_features = (jnp.dot(grad_left, w_left.T, preferred_element_type=jnp.float32) + jnp.dot(grad_right, w_right.T, preferred_element_type=jnp.float32)).astype(jnp.bfloat16)
    grad_w_left = grad_scale * jnp.dot(bin_features.T, grad_left, preferred_element_type=jnp.float32)
    grad_w_right = grad_scale * jnp.dot(bin_features.T, grad_right, preferred_element_type=jnp.float32)
    return (grad_features, grad_w_left, grad_w_right, grad_scale * kern_acc, grad_scale * pointwise_running_sum, grad_scale * head_running_sum)
```

```python
import math

import jax
import jax.numpy as jnp
from jax import lax
from jax.sharding import PartitionSpec as P

DILATION_STEP = 4


def silu_slope(values):
    logistic = jax.nn.sigmoid(values)
    return logistic * (1.0 + values * (1.0 - logistic))


def shifted(x, axis, step, count):
    pairs = [(i, i + step) for i in range(count) if 0 <= i + step < count]
    return lax.ppermute(x, axis, pairs)


def butterfly(values, axis, count):
    bit = 1
    while bit < count:
        pairs = [(i, i ^ bit) for i in range(count)]
        values = jax.tree.map(lambda a, b: a + b, values, lax.ppermute(values, axis, pairs))
        bit *= 2
    return values


def body(bin_features, w_left, w_right, depth_kernel, w_point, w_head, cotangent):
    rows = bin_features.shape[0]
    cols = cotangent.shape[2]
    row_count = lax.axis_size("row")
    col_count = lax.axis_size("col")
    ratio = col_count // row_count
    bins = rows * row_count
    grad_scale = 1.0 / math.sqrt(bins)
    step = DILATION_STEP
    halo = 2 * step
    r = lax.axis_index("row")
    k = lax.axis_index("col")
    part = k % ratio

    left_proj = jnp.dot(bin_features, w_left, preferred_element_type=jnp.float32).astype(jnp.bfloat16)
    right_proj = jnp.dot(bin_features, w_right, preferred_element_type=jnp.float32).astype(jnp.bfloat16)

    cot_rows = jnp.concatenate(
        [
            shifted(cotangent[:, rows - step :, :], "row", 1, row_count),
            cotangent,
            shifted(cotangent[:, :step, :], "row", -1, row_count),
        ],
        axis=1,
    )
    cot_ext = jnp.concatenate(
        [
            shifted(cot_rows[:, :, cols - step :], "col", 1, col_count),
            cot_rows,
            shifted(cot_rows[:, :, :step], "col", -1, col_count),
        ],
        axis=2,
    )

    left_ext = jnp.concatenate(
        [
            shifted(left_proj[rows - halo :], "row", 1, row_count),
            left_proj,
            shifted(left_proj[:halo], "row", -1, row_count),
        ],
        axis=0,
    )

    def target(a, b, shift):
        tile = ratio * a + b % ratio + shift
        return (b // ratio) * col_count + tile if 0 <= tile < col_count else None

    def perm(shift):
        pairs = []
        for a in range(row_count):
            for b in range(col_count):
                t = target(a, b, shift)
                if t is not None:
                    pairs.append((a * col_count + b, t))
        return pairs

    own_tile = lax.dynamic_slice_in_dim(right_proj, part * cols, cols, 0)
    right_main = lax.ppermute(own_tile, ("row", "col"), perm(0))
    right_before = lax.ppermute(own_tile[cols - halo :], ("row", "col"), perm(1))
    right_after = lax.ppermute(own_tile[:halo], ("row", "col"), perm(-1))
    right_ext = jnp.concatenate([right_before, right_main, right_after], axis=0)

    row_place = r * rows - halo + lax.broadcasted_iota(jnp.int32, (rows + 2 * halo, 1), 0)
    col_place = k * cols - halo + lax.broadcasted_iota(jnp.int32, (1, cols + 2 * halo), 1)
    valid = (row_place >= 0) & (row_place < bins) & (col_place >= 0) & (col_place < bins)
    pair_sum = left_ext.astype(jnp.float32).T[:, :, None] + right_ext.astype(jnp.float32).T[:, None, :]
    pair_ext = jnp.where(valid[None], pair_sum, 0.0).astype(jnp.bfloat16)

    ext_rows = rows + 2 * step
    ext_cols = cols + 2 * step
    conv_ext = jnp.zeros((pair_ext.shape[0], ext_rows, ext_cols), jnp.float32)
    for a in range(3):
        for b in range(3):
            conv_ext = conv_ext + depth_kernel[3 * a + b][:, None, None] * pair_ext[
                :, step * a : step * a + ext_rows, step * b : step * b + ext_cols
            ].astype(jnp.float32)
    conv_tile = conv_ext[:, step : step + rows, step : step + cols]
    hidden_state = jax.nn.silu(conv_tile).astype(jnp.bfloat16)
    mixed_out = jnp.einsum("co,cij->oij", w_point, hidden_state, preferred_element_type=jnp.float32)
    pair_tile = pair_ext[:, halo : halo + rows, halo : halo + cols]
    trunk_matrix = (pair_tile.astype(jnp.float32) + mixed_out).astype(jnp.bfloat16)

    trunk_gradient = (
        grad_scale * jnp.einsum("ch,hij->cij", w_head, cot_ext, preferred_element_type=jnp.float32)
    ).astype(jnp.bfloat16)
    grad_hidden = jnp.einsum("co,oij->cij", w_point, trunk_gradient, preferred_element_type=jnp.float32)
    conv_grad = (grad_hidden * silu_slope(conv_ext)).astype(jnp.bfloat16)
    conv_grad_tile = conv_grad[:, step : step + rows, step : step + cols].astype(jnp.float32)
    trunk_grad_tile = trunk_gradient[:, step : step + rows, step : step + cols]

    backward_pass = trunk_grad_tile.astype(jnp.float32)
    kern_terms = []
    for a in range(3):
        for b in range(3):
            backward_pass = backward_pass + depth_kernel[3 * a + b][:, None, None] * conv_grad[
                :, step * (2 - a) : step * (2 - a) + rows, step * (2 - b) : step * (2 - b) + cols
            ].astype(jnp.float32)
            window = pair_ext[
                :, step + step * a : step + step * a + rows, step + step * b : step + step * b + cols
            ].astype(jnp.float32)
            kern_terms.append(jnp.sum(conv_grad_tile * window, axis=(1, 2)))
    kernel_part = jnp.stack(kern_terms)
    left_part = jnp.sum(backward_pass, axis=2).T
    right_part = jnp.sum(backward_pass, axis=1).T
    point_part = jnp.einsum(
        "fsk,gsk->fg", hidden_state, trunk_grad_tile, preferred_element_type=jnp.float32
    )
    head_part = jnp.einsum("ydq,gdq->yg", trunk_matrix, cotangent, preferred_element_type=jnp.float32)
    small = jnp.concatenate([kernel_part.ravel(), point_part.ravel(), head_part.ravel()])

    left_total, small = butterfly((left_part, small), "col", col_count)
    column_total = butterfly(right_part, "row", row_count)

    def redistribute(shift):
        pairs = []
        for a in range(row_count):
            for b in range(col_count):
                src = (b // ratio) * col_count + ratio * a + (b % ratio + shift) % ratio
                pairs.append((src, a * col_count + b))
        return lax.ppermute(column_total, ("row", "col"), pairs)

    received = jnp.stack([redistribute(q) for q in range(ratio)])
    grad_right = jnp.concatenate(
        [received[(m - part) % ratio] for m in range(ratio)], axis=0
    ).astype(jnp.bfloat16)
    grad_left = left_total.astype(jnp.bfloat16)

    grad_features = (
        jnp.dot(grad_left, w_left.T, preferred_element_type=jnp.float32)
        + jnp.dot(grad_right, w_right.T, preferred_element_type=jnp.float32)
    ).astype(jnp.bfloat16)
    contract = (((0,), (0,)), ((), ()))
    wleft_part = lax.dot_general(bin_features, grad_left, contract, preferred_element_type=jnp.float32)
    wright_part = lax.dot_general(bin_features, grad_right, contract, preferred_element_type=jnp.float32)
    wleft_sum, wright_sum, small = butterfly((wleft_part, wright_part, small), "row", row_count)

    chans = w_left.shape[1]
    heads = w_head.shape[1]
    taps = kernel_part.size
    kernel_sum = small[:taps].reshape(kernel_part.shape)
    point_sum = small[taps : taps + chans * chans].reshape(chans, chans)
    head_sum = small[taps + chans * chans :].reshape(chans, heads)
    return (
        grad_features,
        grad_scale * wleft_sum,
        grad_scale * wright_sum,
        grad_scale * kernel_sum,
        grad_scale * point_sum,
        grad_scale * head_sum,
    )


def solution(mesh):
    placed = (P("row", None), P(), P(), P(), P(), P(), P(None, "row", "col"))
    return jax.shard_map(
        body,
        mesh=mesh,
        in_specs=placed,
        out_specs=(P("row", None), P(), P(), P(), P(), P()),
        check_vma=False,
    )
```

```python
import math

import jax
import jax.numpy as jnp
from jax import lax
from jax.sharding import PartitionSpec as P

DILATION_STEP = 4


def silu_slope(values):
    logistic = jax.nn.sigmoid(values)
    return logistic * (1.0 + values * (1.0 - logistic))


def shifted(x, axis, step, count):
    pairs = [(i, i + step) for i in range(count) if 0 <= i + step < count]
    return lax.ppermute(x, axis, pairs)


def packed(parts):
    return jnp.concatenate([p.ravel() for p in parts])


def unpacked(flat, likes):
    out, at = [], 0
    for like in likes:
        out.append(flat[at : at + like.size].reshape(like.shape))
        at += like.size
    return out


def xor_round(flat, axis, count, bit):
    return lax.ppermute(flat, axis, [(i, i ^ bit) for i in range(count)])


def body(bin_features, w_left, w_right, depth_kernel, w_point, w_head, cotangent):
    rows = bin_features.shape[0]
    cols = cotangent.shape[2]
    row_count = lax.axis_size("row")
    col_count = lax.axis_size("col")
    ratio = col_count // row_count
    bins = rows * row_count
    grad_scale = 1.0 / math.sqrt(bins)
    step = DILATION_STEP
    halo = 2 * step
    r = lax.axis_index("row")
    k = lax.axis_index("col")
    part = k % ratio

    left_proj = jnp.dot(bin_features, w_left, preferred_element_type=jnp.float32).astype(jnp.bfloat16)
    right_proj = jnp.dot(bin_features, w_right, preferred_element_type=jnp.float32).astype(jnp.bfloat16)

    tail = (cotangent[:, rows - step :, :], left_proj[rows - halo :], right_proj[rows - halo :])
    head = (cotangent[:, :step, :], left_proj[:halo], right_proj[:halo])
    before = unpacked(shifted(packed(tail), "row", 1, row_count), tail)
    after = unpacked(shifted(packed(head), "row", -1, row_count), head)
    cot_rows = jnp.concatenate([before[0], cotangent, after[0]], axis=1)
    left_ext = jnp.concatenate([before[1], left_proj, after[1]], axis=0)
    right_panel = jnp.concatenate([before[2], right_proj, after[2]], axis=0)
    cot_ext = jnp.concatenate(
        [
            shifted(cot_rows[:, :, cols - step :], "col", 1, col_count),
            cot_rows,
            shifted(cot_rows[:, :, :step], "col", -1, col_count),
        ],
        axis=2,
    )

    def transpose_pairs():
        pairs = []
        for a in range(row_count):
            for b in range(col_count):
                pairs.append((a * col_count + b, (b // ratio) * col_count + ratio * a + b % ratio))
        return pairs

    own_tile = lax.dynamic_slice_in_dim(right_panel, part * cols, cols + 2 * halo, 0)
    right_ext = lax.ppermute(own_tile, ("row", "col"), transpose_pairs())

    row_place = r * rows - halo + lax.broadcasted_iota(jnp.int32, (rows + 2 * halo, 1), 0)
    col_place = k * cols - halo + lax.broadcasted_iota(jnp.int32, (1, cols + 2 * halo), 1)
    valid = (row_place >= 0) & (row_place < bins) & (col_place >= 0) & (col_place < bins)
    pair_sum = left_ext.astype(jnp.float32).T[:, :, None] + right_ext.astype(jnp.float32).T[:, None, :]
    pair_ext = jnp.where(valid[None], pair_sum, 0.0).astype(jnp.bfloat16)

    ext_rows = rows + 2 * step
    ext_cols = cols + 2 * step
    conv_ext = jnp.zeros((pair_ext.shape[0], ext_rows, ext_cols), jnp.float32)
    for a in range(3):
        for b in range(3):
            conv_ext = conv_ext + depth_kernel[3 * a + b][:, None, None] * pair_ext[
                :, step * a : step * a + ext_rows, step * b : step * b + ext_cols
            ].astype(jnp.float32)
    conv_tile = conv_ext[:, step : step + rows, step : step + cols]
    hidden_state = jax.nn.silu(conv_tile).astype(jnp.bfloat16)
    mixed_out = jnp.einsum("co,cij->oij", w_point, hidden_state, preferred_element_type=jnp.float32)
    pair_tile = pair_ext[:, halo : halo + rows, halo : halo + cols]
    trunk_matrix = (pair_tile.astype(jnp.float32) + mixed_out).astype(jnp.bfloat16)

    trunk_gradient = (
        grad_scale * jnp.einsum("ch,hij->cij", w_head, cot_ext, preferred_element_type=jnp.float32)
    ).astype(jnp.bfloat16)
    grad_hidden = jnp.einsum("co,oij->cij", w_point, trunk_gradient, preferred_element_type=jnp.float32)
    conv_grad = (grad_hidden * silu_slope(conv_ext)).astype(jnp.bfloat16)
    conv_grad_tile = conv_grad[:, step : step + rows, step : step + cols].astype(jnp.float32)
    trunk_grad_tile = trunk_gradient[:, step : step + rows, step : step + cols]

    backward_pass = trunk_grad_tile.astype(jnp.float32)
    kern_terms = []
    for a in range(3):
        for b in range(3):
            backward_pass = backward_pass + depth_kernel[3 * a + b][:, None, None] * conv_grad[
                :, step * (2 - a) : step * (2 - a) + rows, step * (2 - b) : step * (2 - b) + cols
            ].astype(jnp.float32)
            window = pair_ext[
                :, step + step * a : step + step * a + rows, step + step * b : step + step * b + cols
            ].astype(jnp.float32)
            kern_terms.append(jnp.sum(conv_grad_tile * window, axis=(1, 2)))
    kernel_part = jnp.stack(kern_terms)
    left_part = jnp.sum(backward_pass, axis=2).T
    right_part = jnp.sum(backward_pass, axis=1).T
    point_part = jnp.einsum(
        "fsk,gsk->fg", hidden_state, trunk_grad_tile, preferred_element_type=jnp.float32
    )
    head_part = jnp.einsum("ydq,gdq->yg", trunk_matrix, cotangent, preferred_element_type=jnp.float32)
    small = packed((kernel_part, point_part, head_part))

    right_moved = lax.ppermute(right_part, ("row", "col"), transpose_pairs())
    bit = ratio
    while bit < col_count:
        likes = (left_part, right_moved, small)
        flat = packed(likes)
        left_part, right_moved, small = unpacked(flat + xor_round(flat, "col", col_count, bit), likes)
        bit *= 2
    right_block = right_moved
    bit = 1
    while bit < ratio:
        likes = (left_part, right_block, small)
        flat = packed(likes)
        got = unpacked(xor_round(flat, "col", col_count, bit), likes)
        left_part = left_part + got[0]
        small = small + got[2]
        upper = (k & bit) != 0
        right_block = jnp.concatenate(
            [jnp.where(upper, got[1], right_block), jnp.where(upper, right_block, got[1])], axis=0
        )
        bit *= 2
    grad_left = left_part.astype(jnp.bfloat16)
    grad_right = right_block.astype(jnp.bfloat16)

    grad_features = (
        jnp.dot(grad_left, w_left.T, preferred_element_type=jnp.float32)
        + jnp.dot(grad_right, w_right.T, preferred_element_type=jnp.float32)
    ).astype(jnp.bfloat16)
    contract = (((0,), (0,)), ((), ()))
    wleft_part = lax.dot_general(bin_features, grad_left, contract, preferred_element_type=jnp.float32)
    wright_part = lax.dot_general(bin_features, grad_right, contract, preferred_element_type=jnp.float32)
    bit = 1
    while bit < row_count:
        likes = (wleft_part, wright_part, small)
        flat = packed(likes)
        wleft_part, wright_part, small = unpacked(flat + xor_round(flat, "row", row_count, bit), likes)
        bit *= 2

    kernel_sum, point_sum, head_sum = unpacked(small, (kernel_part, point_part, head_part))
    return (
        grad_features,
        grad_scale * wleft_part,
        grad_scale * wright_part,
        grad_scale * kernel_sum,
        grad_scale * point_sum,
        grad_scale * head_sum,
    )


def solution(mesh):
    placed = (P("row", None), P(), P(), P(), P(), P(), P(None, "row", "col"))
    return jax.shard_map(
        body,
        mesh=mesh,
        in_specs=placed,
        out_specs=(P("row", None), P(), P(), P(), P(), P()),
        check_vma=False,
    )
```

```python
import math

import jax
import jax.numpy as jnp
from jax import lax
from jax.experimental import pallas as pl
from jax.experimental.pallas import tpu as pltpu
from jax.sharding import PartitionSpec as P

DILATION_STEP = 4
LANES = 256
FWD = 24
BWD = 32


def silu_slope(values):
    logistic = jax.nn.sigmoid(values)
    return logistic * (1.0 + values * (1.0 - logistic))


def shift_left(x, n):
    return x if n == 0 else pltpu.roll(x, LANES - n, 1)


def depth_kernel_body(taps_ref, pair_ref, gh_ref, gt_ref, hid_ref, gp_ref, kern_ref, pair_s, gh_s, conv_s, gc_s):
    c = pl.program_id(0)
    chans = pl.num_programs(0)
    pcol = pair_ref.shape[2]
    erow, ecol = gh_ref.shape[1], gh_ref.shape[2]
    rows, cols = gt_ref.shape[1], gt_ref.shape[2]
    tap = [taps_ref[t * chans + c] for t in range(9)]
    pair_s[...] = jnp.zeros_like(pair_s)
    pair_s[:, :pcol] = pair_ref[0].astype(jnp.float32)
    gh_s[...] = jnp.zeros_like(gh_s)
    gh_s[:, :ecol] = gh_ref[0]

    def forward(s, carry):
        conv = None
        for a in range(3):
            window = pair_s[pl.ds(FWD * s + DILATION_STEP * a, FWD), :]
            for b in range(3):
                term = tap[3 * a + b] * shift_left(window, DILATION_STEP * b)
                conv = term if conv is None else conv + term
        at = FWD * s
        conv_s[pl.ds(at, FWD), :] = conv
        gc = gh_s[pl.ds(at, FWD), :] * silu_slope(conv)
        gc_s[pl.ds(at, FWD), :] = gc.astype(jnp.bfloat16).astype(jnp.float32)
        return carry

    for s in range(erow // FWD):
        forward(s, 0)

    def backward(s, sums):
        at = BWD * s
        conv_tile = shift_left(conv_s[pl.ds(at + DILATION_STEP, BWD), :], DILATION_STEP)[:, :cols]
        hid_ref[0, pl.ds(at, BWD), :] = jax.nn.silu(conv_tile).astype(hid_ref.dtype)
        gc_tile = shift_left(gc_s[pl.ds(at + DILATION_STEP, BWD), :], DILATION_STEP)[:, :cols]
        grad = gt_ref[0, pl.ds(at, BWD), :].astype(jnp.float32)
        out = []
        for a in range(3):
            gc_rows = gc_s[pl.ds(at + DILATION_STEP * (2 - a), BWD), :]
            pair_rows = pair_s[pl.ds(at + DILATION_STEP + DILATION_STEP * a, BWD), :]
            for b in range(3):
                grad = grad + tap[3 * a + b] * shift_left(gc_rows, DILATION_STEP * (2 - b))[:, :cols]
                window = shift_left(pair_rows, DILATION_STEP + DILATION_STEP * b)[:, :cols]
                out.append(sums[3 * a + b] + gc_tile * window)
        gp_ref[0, pl.ds(at, BWD), :] = grad
        return tuple(out)

    zero = jnp.zeros((BWD, cols), jnp.float32)
    sums = (zero,) * 9
    for s in range(rows // BWD):
        sums = backward(s, sums)
    for t in range(9):
        kern_ref[0, pl.ds(t, 1), :] = jnp.sum(sums[t], axis=0, keepdims=True)


def depth_call(taps, pair_ext, grad_hidden, trunk_grad_tile):
    chans, prow, pcol = pair_ext.shape
    _, erow, ecol = grad_hidden.shape
    _, rows, cols = trunk_grad_tile.shape
    return pl.pallas_call(
        depth_kernel_body,
        grid=(chans,),
        in_specs=[
            pl.BlockSpec(memory_space=pltpu.SMEM),
            pl.BlockSpec((1, prow, pcol), lambda c: (c, 0, 0)),
            pl.BlockSpec((1, erow, ecol), lambda c: (c, 0, 0)),
            pl.BlockSpec((1, rows, cols), lambda c: (c, 0, 0)),
        ],
        out_specs=[
            pl.BlockSpec((1, rows, cols), lambda c: (c, 0, 0)),
            pl.BlockSpec((1, rows, cols), lambda c: (c, 0, 0)),
            pl.BlockSpec((1, 9, cols), lambda c: (c, 0, 0)),
        ],
        out_shape=[
            jax.ShapeDtypeStruct((chans, rows, cols), jnp.bfloat16),
            jax.ShapeDtypeStruct((chans, rows, cols), jnp.float32),
            jax.ShapeDtypeStruct((chans, 9, cols), jnp.float32),
        ],
        scratch_shapes=[
            pltpu.VMEM((prow, LANES), jnp.float32),
            pltpu.VMEM((erow, LANES), jnp.float32),
            pltpu.VMEM((erow, LANES), jnp.float32),
            pltpu.VMEM((erow, LANES), jnp.float32),
        ],
    )(taps.ravel(), pair_ext, grad_hidden, trunk_grad_tile)


def shifted(x, axis, step, count):
    pairs = [(i, i + step) for i in range(count) if 0 <= i + step < count]
    return lax.ppermute(x, axis, pairs)


def packed(parts):
    return jnp.concatenate([p.ravel() for p in parts])


def unpacked(flat, likes):
    out, at = [], 0
    for like in likes:
        out.append(flat[at : at + like.size].reshape(like.shape))
        at += like.size
    return out


def xor_round(flat, axis, count, bit):
    return lax.ppermute(flat, axis, [(i, i ^ bit) for i in range(count)])


def body(bin_features, w_left, w_right, depth_kernel, w_point, w_head, cotangent):
    rows = bin_features.shape[0]
    cols = cotangent.shape[2]
    row_count = lax.axis_size("row")
    col_count = lax.axis_size("col")
    ratio = col_count // row_count
    bins = rows * row_count
    grad_scale = 1.0 / math.sqrt(bins)
    step = DILATION_STEP
    halo = 2 * step
    r = lax.axis_index("row")
    k = lax.axis_index("col")
    part = k % ratio

    left_proj = jnp.dot(bin_features, w_left, preferred_element_type=jnp.float32).astype(jnp.bfloat16)
    right_proj = jnp.dot(bin_features, w_right, preferred_element_type=jnp.float32).astype(jnp.bfloat16)

    tail = (cotangent[:, rows - step :, :], left_proj[rows - halo :], right_proj[rows - halo :])
    head = (cotangent[:, :step, :], left_proj[:halo], right_proj[:halo])
    before = unpacked(shifted(packed(tail), "row", 1, row_count), tail)
    after = unpacked(shifted(packed(head), "row", -1, row_count), head)
    cot_rows = jnp.concatenate([before[0], cotangent, after[0]], axis=1)
    left_ext = jnp.concatenate([before[1], left_proj, after[1]], axis=0)
    right_panel = jnp.concatenate([before[2], right_proj, after[2]], axis=0)
    cot_ext = jnp.concatenate(
        [
            shifted(cot_rows[:, :, cols - step :], "col", 1, col_count),
            cot_rows,
            shifted(cot_rows[:, :, :step], "col", -1, col_count),
        ],
        axis=2,
    )

    def transpose_pairs():
        pairs = []
        for a in range(row_count):
            for b in range(col_count):
                pairs.append((a * col_count + b, (b // ratio) * col_count + ratio * a + b % ratio))
        return pairs

    own_tile = lax.dynamic_slice_in_dim(right_panel, part * cols, cols + 2 * halo, 0)
    right_ext = lax.ppermute(own_tile, ("row", "col"), transpose_pairs())

    row_place = r * rows - halo + lax.broadcasted_iota(jnp.int32, (rows + 2 * halo, 1), 0)
    col_place = k * cols - halo + lax.broadcasted_iota(jnp.int32, (1, cols + 2 * halo), 1)
    valid = (row_place >= 0) & (row_place < bins) & (col_place >= 0) & (col_place < bins)
    pair_sum = left_ext.astype(jnp.float32).T[:, :, None] + right_ext.astype(jnp.float32).T[:, None, :]
    pair_ext = jnp.where(valid[None], pair_sum, 0.0).astype(jnp.bfloat16)

    trunk_gradient = (
        grad_scale * jnp.einsum("ch,hij->cij", w_head, cot_ext, preferred_element_type=jnp.float32)
    ).astype(jnp.bfloat16)
    grad_hidden = jnp.einsum("co,oij->cij", w_point, trunk_gradient, preferred_element_type=jnp.float32)
    trunk_grad_tile = trunk_gradient[:, step : step + rows, step : step + cols]
    hidden_state, backward_pass, kern_rows = depth_call(depth_kernel, pair_ext, grad_hidden, trunk_grad_tile)
    mixed_out = jnp.einsum("co,cij->oij", w_point, hidden_state, preferred_element_type=jnp.float32)
    pair_tile = pair_ext[:, halo : halo + rows, halo : halo + cols]
    trunk_matrix = (pair_tile.astype(jnp.float32) + mixed_out).astype(jnp.bfloat16)
    kernel_part = jnp.sum(kern_rows, axis=2).T
    left_part = jnp.sum(backward_pass, axis=2).T
    right_part = jnp.sum(backward_pass, axis=1).T
    point_part = jnp.einsum(
        "fsk,gsk->fg", hidden_state, trunk_grad_tile, preferred_element_type=jnp.float32
    )
    head_part = jnp.einsum("ydq,gdq->yg", trunk_matrix, cotangent, preferred_element_type=jnp.float32)
    small = packed((kernel_part, point_part, head_part))

    right_moved = lax.ppermute(right_part, ("row", "col"), transpose_pairs())
    bit = ratio
    while bit < col_count:
        likes = (left_part, right_moved, small)
        flat = packed(likes)
        left_part, right_moved, small = unpacked(flat + xor_round(flat, "col", col_count, bit), likes)
        bit *= 2
    right_block = right_moved
    bit = 1
    while bit < ratio:
        likes = (left_part, right_block, small)
        flat = packed(likes)
        got = unpacked(xor_round(flat, "col", col_count, bit), likes)
        left_part = left_part + got[0]
        small = small + got[2]
        upper = (k & bit) != 0
        right_block = jnp.concatenate(
            [jnp.where(upper, got[1], right_block), jnp.where(upper, right_block, got[1])], axis=0
        )
        bit *= 2
    grad_left = left_part.astype(jnp.bfloat16)
    grad_right = right_block.astype(jnp.bfloat16)

    grad_features = (
        jnp.dot(grad_left, w_left.T, preferred_element_type=jnp.float32)
        + jnp.dot(grad_right, w_right.T, preferred_element_type=jnp.float32)
    ).astype(jnp.bfloat16)
    contract = (((0,), (0,)), ((), ()))
    wleft_part = lax.dot_general(bin_features, grad_left, contract, preferred_element_type=jnp.float32)
    wright_part = lax.dot_general(bin_features, grad_right, contract, preferred_element_type=jnp.float32)
    bit = 1
    while bit < row_count:
        likes = (wleft_part, wright_part, small)
        flat = packed(likes)
        wleft_part, wright_part, small = unpacked(flat + xor_round(flat, "row", row_count, bit), likes)
        bit *= 2

    kernel_sum, point_sum, head_sum = unpacked(small, (kernel_part, point_part, head_part))
    return (
        grad_features,
        grad_scale * wleft_part,
        grad_scale * wright_part,
        grad_scale * kernel_sum,
        grad_scale * point_sum,
        grad_scale * head_sum,
    )


def solution(mesh):
    placed = (P("row", None), P(), P(), P(), P(), P(), P(None, "row", "col"))
    return jax.shard_map(
        body,
        mesh=mesh,
        in_specs=placed,
        out_specs=(P("row", None), P(), P(), P(), P(), P()),
        check_vma=False,
    )
```

```python
import math

import jax
import jax.numpy as jnp
from jax import lax
from jax.sharding import PartitionSpec as P

DILATION_STEP = 4


def silu_slope(values):
    logistic = jax.nn.sigmoid(values)
    return logistic * (1.0 + values * (1.0 - logistic))


def shifted(x, axis, step, count):
    pairs = [(i, i + step) for i in range(count) if 0 <= i + step < count]
    return lax.ppermute(x, axis, pairs)


def packed(parts):
    return jnp.concatenate([p.ravel() for p in parts])


def unpacked(flat, likes):
    out, at = [], 0
    for like in likes:
        out.append(flat[at : at + like.size].reshape(like.shape))
        at += like.size
    return out


def xor_round(flat, axis, count, bit):
    return lax.ppermute(flat, axis, [(i, i ^ bit) for i in range(count)])


def body(bin_features, w_left, w_right, depth_kernel, w_point, w_head, cotangent):
    rows = bin_features.shape[0]
    cols = cotangent.shape[2]
    row_count = lax.axis_size("row")
    col_count = lax.axis_size("col")
    ratio = col_count // row_count
    bins = rows * row_count
    grad_scale = 1.0 / math.sqrt(bins)
    step = DILATION_STEP
    halo = 2 * step
    r = lax.axis_index("row")
    k = lax.axis_index("col")
    part = k % ratio

    left_proj = jnp.dot(bin_features, w_left, preferred_element_type=jnp.float32).astype(jnp.bfloat16)
    right_proj = jnp.dot(bin_features, w_right, preferred_element_type=jnp.float32).astype(jnp.bfloat16)

    tail = (cotangent[:, rows - step :, :], left_proj[rows - halo :])
    head = (cotangent[:, :step, :], left_proj[:halo])
    before = unpacked(shifted(packed(tail), "row", 1, row_count), tail)
    after = unpacked(shifted(packed(head), "row", -1, row_count), head)
    cot_rows = jnp.concatenate([before[0], cotangent, after[0]], axis=1)
    left_ext = jnp.concatenate([before[1], left_proj, after[1]], axis=0)
    cot_ext = jnp.concatenate(
        [
            shifted(cot_rows[:, :, cols - step :], "col", 1, col_count),
            cot_rows,
            shifted(cot_rows[:, :, :step], "col", -1, col_count),
        ],
        axis=2,
    )

    def transpose_pairs(shift=0):
        pairs = []
        for a in range(row_count):
            for b in range(col_count):
                tile = ratio * a + b % ratio + shift
                if 0 <= tile < col_count:
                    pairs.append((a * col_count + b, (b // ratio) * col_count + tile))
        return pairs

    own_tile = lax.dynamic_slice_in_dim(right_proj, part * cols, cols, 0)
    right_ext = jnp.concatenate(
        [
            lax.ppermute(own_tile[cols - halo :], ("row", "col"), transpose_pairs(1)),
            lax.ppermute(own_tile, ("row", "col"), transpose_pairs()),
            lax.ppermute(own_tile[:halo], ("row", "col"), transpose_pairs(-1)),
        ],
        axis=0,
    )

    row_place = r * rows - halo + lax.broadcasted_iota(jnp.int32, (rows + 2 * halo, 1), 0)
    col_place = k * cols - halo + lax.broadcasted_iota(jnp.int32, (1, cols + 2 * halo), 1)
    valid = (row_place >= 0) & (row_place < bins) & (col_place >= 0) & (col_place < bins)
    pair_sum = left_ext.astype(jnp.float32).T[:, :, None] + right_ext.astype(jnp.float32).T[:, None, :]
    pair_ext = jnp.where(valid[None], pair_sum, 0.0).astype(jnp.bfloat16)

    ext_rows = rows + 2 * step
    ext_cols = cols + 2 * step
    conv_ext = jnp.zeros((pair_ext.shape[0], ext_rows, ext_cols), jnp.float32)
    for a in range(3):
        for b in range(3):
            conv_ext = conv_ext + depth_kernel[3 * a + b][:, None, None] * pair_ext[
                :, step * a : step * a + ext_rows, step * b : step * b + ext_cols
            ].astype(jnp.float32)
    conv_tile = conv_ext[:, step : step + rows, step : step + cols]
    hidden_state = jax.nn.silu(conv_tile).astype(jnp.bfloat16)
    mixed_out = jnp.einsum("co,cij->oij", w_point, hidden_state, preferred_element_type=jnp.float32)
    pair_tile = pair_ext[:, halo : halo + rows, halo : halo + cols]
    trunk_matrix = (pair_tile.astype(jnp.float32) + mixed_out).astype(jnp.bfloat16)

    trunk_gradient = (
        grad_scale * jnp.einsum("ch,hij->cij", w_head, cot_ext, preferred_element_type=jnp.float32)
    ).astype(jnp.bfloat16)
    grad_hidden = jnp.einsum("co,oij->cij", w_point, trunk_gradient, preferred_element_type=jnp.float32)
    conv_grad = (grad_hidden * silu_slope(conv_ext)).astype(jnp.bfloat16)
    conv_grad_tile = conv_grad[:, step : step + rows, step : step + cols].astype(jnp.float32)
    trunk_grad_tile = trunk_gradient[:, step : step + rows, step : step + cols]

    backward_pass = trunk_grad_tile.astype(jnp.float32)
    kern_terms = []
    for a in range(3):
        for b in range(3):
            backward_pass = backward_pass + depth_kernel[3 * a + b][:, None, None] * conv_grad[
                :, step * (2 - a) : step * (2 - a) + rows, step * (2 - b) : step * (2 - b) + cols
            ].astype(jnp.float32)
            window = pair_ext[
                :, step + step * a : step + step * a + rows, step + step * b : step + step * b + cols
            ].astype(jnp.float32)
            kern_terms.append(jnp.sum(conv_grad_tile * window, axis=(1, 2)))
    kernel_part = jnp.stack(kern_terms)
    left_part = jnp.sum(backward_pass, axis=2).T
    right_part = jnp.sum(backward_pass, axis=1).T
    point_part = jnp.einsum(
        "fsk,gsk->fg", hidden_state, trunk_grad_tile, preferred_element_type=jnp.float32
    )
    head_part = jnp.einsum("ydq,gdq->yg", trunk_matrix, cotangent, preferred_element_type=jnp.float32)
    small = packed((kernel_part, point_part, head_part))

    right_moved = lax.ppermute(right_part, ("row", "col"), transpose_pairs())
    bit = ratio
    while bit < col_count:
        likes = (left_part, right_moved, small)
        flat = packed(likes)
        left_part, right_moved, small = unpacked(flat + xor_round(flat, "col", col_count, bit), likes)
        bit *= 2
    right_block = right_moved
    bit = 1
    while bit < ratio:
        likes = (left_part, right_block, small)
        flat = packed(likes)
        got = unpacked(xor_round(flat, "col", col_count, bit), likes)
        left_part = left_part + got[0]
        small = small + got[2]
        upper = (k & bit) != 0
        right_block = jnp.concatenate(
            [jnp.where(upper, got[1], right_block), jnp.where(upper, right_block, got[1])], axis=0
        )
        bit *= 2
    grad_left = left_part.astype(jnp.bfloat16)
    grad_right = right_block.astype(jnp.bfloat16)

    grad_features = (
        jnp.dot(grad_left, w_left.T, preferred_element_type=jnp.float32)
        + jnp.dot(grad_right, w_right.T, preferred_element_type=jnp.float32)
    ).astype(jnp.bfloat16)
    contract = (((0,), (0,)), ((), ()))
    wleft_part = lax.dot_general(bin_features, grad_left, contract, preferred_element_type=jnp.float32)
    wright_part = lax.dot_general(bin_features, grad_right, contract, preferred_element_type=jnp.float32)
    bit = 1
    while bit < row_count:
        likes = (wleft_part, wright_part, small)
        flat = packed(likes)
        wleft_part, wright_part, small = unpacked(flat + xor_round(flat, "row", row_count, bit), likes)
        bit *= 2

    kernel_sum, point_sum, head_sum = unpacked(small, (kernel_part, point_part, head_part))
    return (
        grad_features,
        grad_scale * wleft_part,
        grad_scale * wright_part,
        grad_scale * kernel_sum,
        grad_scale * point_sum,
        grad_scale * head_sum,
    )


def solution(mesh):
    placed = (P("row", None), P(), P(), P(), P(), P(), P(None, "row", "col"))
    return jax.shard_map(
        body,
        mesh=mesh,
        in_specs=placed,
        out_specs=(P("row", None), P(), P(), P(), P(), P()),
        check_vma=False,
    )
```

```python
import math

import jax
import jax.numpy as jnp
from jax import lax
from jax.sharding import PartitionSpec as P

DILATION_STEP = 4


def silu_slope(values):
    logistic = jax.nn.sigmoid(values)
    return logistic * (1.0 + values * (1.0 - logistic))


def shifted(x, axis, step, count):
    pairs = [(i, i + step) for i in range(count) if 0 <= i + step < count]
    return lax.ppermute(x, axis, pairs)


def packed(parts):
    return jnp.concatenate([p.ravel() for p in parts])


def unpacked(flat, likes):
    out, at = [], 0
    for like in likes:
        out.append(flat[at : at + like.size].reshape(like.shape))
        at += like.size
    return out


def xor_round(flat, axis, count, bit):
    return lax.ppermute(flat, axis, [(i, i ^ bit) for i in range(count)])


def body(bin_features, w_left, w_right, depth_kernel, w_point, w_head, cotangent):
    rows = bin_features.shape[0]
    cols = cotangent.shape[2]
    row_count = lax.axis_size("row")
    col_count = lax.axis_size("col")
    ratio = col_count // row_count
    bins = rows * row_count
    grad_scale = 1.0 / math.sqrt(bins)
    step = DILATION_STEP
    halo = 2 * step
    r = lax.axis_index("row")
    k = lax.axis_index("col")
    part = k % ratio

    left_proj = jnp.dot(bin_features, w_left, preferred_element_type=jnp.float32).astype(jnp.bfloat16)
    right_proj = jnp.dot(bin_features, w_right, preferred_element_type=jnp.float32).astype(jnp.bfloat16)

    tail = (cotangent[:, rows - step :, :], left_proj[rows - halo :], right_proj[rows - halo :])
    head = (cotangent[:, :step, :], left_proj[:halo], right_proj[:halo])
    before = unpacked(shifted(packed(tail), "row", 1, row_count), tail)
    after = unpacked(shifted(packed(head), "row", -1, row_count), head)
    cot_rows = jnp.concatenate([before[0], cotangent, after[0]], axis=1)
    left_ext = jnp.concatenate([before[1], left_proj, after[1]], axis=0)
    right_panel = jnp.concatenate([before[2], right_proj, after[2]], axis=0)
    cot_strips = (
        shifted(cot_rows[:, :, cols - step :], "col", 1, col_count),
        cot_rows,
        shifted(cot_rows[:, :, :step], "col", -1, col_count),
    )

    def transpose_pairs():
        pairs = []
        for a in range(row_count):
            for b in range(col_count):
                pairs.append((a * col_count + b, (b // ratio) * col_count + ratio * a + b % ratio))
        return pairs

    own_tile = lax.dynamic_slice_in_dim(right_panel, part * cols, cols + 2 * halo, 0)
    right_ext = lax.ppermute(own_tile, ("row", "col"), transpose_pairs())

    row_place = r * rows - halo + lax.broadcasted_iota(jnp.int32, (rows + 2 * halo, 1), 0)
    col_place = k * cols - halo + lax.broadcasted_iota(jnp.int32, (1, cols + 2 * halo), 1)
    valid = (row_place >= 0) & (row_place < bins) & (col_place >= 0) & (col_place < bins)
    pair_sum = left_ext.astype(jnp.float32).T[:, :, None] + right_ext.astype(jnp.float32).T[:, None, :]
    pair_ext = jnp.where(valid[None], pair_sum, 0.0).astype(jnp.bfloat16)

    ext_rows = rows + 2 * step
    ext_cols = cols + 2 * step
    conv_ext = jnp.zeros((pair_ext.shape[0], ext_rows, ext_cols), jnp.float32)
    for a in range(3):
        for b in range(3):
            conv_ext = conv_ext + depth_kernel[3 * a + b][:, None, None] * pair_ext[
                :, step * a : step * a + ext_rows, step * b : step * b + ext_cols
            ].astype(jnp.float32)
    conv_tile = conv_ext[:, step : step + rows, step : step + cols]
    hidden_state = jax.nn.silu(conv_tile).astype(jnp.bfloat16)
    mixed_out = jnp.einsum("co,cij->oij", w_point, hidden_state, preferred_element_type=jnp.float32)
    pair_tile = pair_ext[:, halo : halo + rows, halo : halo + cols]
    trunk_matrix = (pair_tile.astype(jnp.float32) + mixed_out).astype(jnp.bfloat16)

    trunk_strips = [
        (
            grad_scale * jnp.einsum("ch,hij->cij", w_head, strip, preferred_element_type=jnp.float32)
        ).astype(jnp.bfloat16)
        for strip in cot_strips
    ]
    trunk_gradient = jnp.concatenate(trunk_strips, axis=2)
    grad_hidden = jnp.concatenate(
        [
            jnp.einsum("co,oij->cij", w_point, strip, preferred_element_type=jnp.float32)
            for strip in trunk_strips
        ],
        axis=2,
    )
    conv_grad = (grad_hidden * silu_slope(conv_ext)).astype(jnp.bfloat16)
    conv_grad_tile = conv_grad[:, step : step + rows, step : step + cols].astype(jnp.float32)
    trunk_grad_tile = trunk_gradient[:, step : step + rows, step : step + cols]

    backward_pass = trunk_grad_tile.astype(jnp.float32)
    kern_terms = []
    for a in range(3):
        for b in range(3):
            backward_pass = backward_pass + depth_kernel[3 * a + b][:, None, None] * conv_grad[
                :, step * (2 - a) : step * (2 - a) + rows, step * (2 - b) : step * (2 - b) + cols
            ].astype(jnp.float32)
            window = pair_ext[
                :, step + step * a : step + step * a + rows, step + step * b : step + step * b + cols
            ].astype(jnp.float32)
            kern_terms.append(jnp.sum(conv_grad_tile * window, axis=(1, 2)))
    kernel_part = jnp.stack(kern_terms)
    left_part = jnp.sum(backward_pass, axis=2).T
    right_part = jnp.sum(backward_pass, axis=1).T
    point_part = jnp.einsum(
        "fsk,gsk->fg", hidden_state, trunk_grad_tile, preferred_element_type=jnp.float32
    )
    head_part = jnp.einsum("ydq,gdq->yg", trunk_matrix, cotangent, preferred_element_type=jnp.float32)
    small = packed((kernel_part, point_part, head_part))

    right_moved = lax.ppermute(right_part, ("row", "col"), transpose_pairs())
    bit = ratio
    while bit < col_count:
        likes = (left_part, right_moved, small)
        flat = packed(likes)
        left_part, right_moved, small = unpacked(flat + xor_round(flat, "col", col_count, bit), likes)
        bit *= 2
    right_block = right_moved
    bit = 1
    while bit < ratio:
        likes = (left_part, right_block, small)
        flat = packed(likes)
        got = unpacked(xor_round(flat, "col", col_count, bit), likes)
        left_part = left_part + got[0]
        small = small + got[2]
        upper = (k & bit) != 0
        right_block = jnp.concatenate(
            [jnp.where(upper, got[1], right_block), jnp.where(upper, right_block, got[1])], axis=0
        )
        bit *= 2
    grad_left = left_part.astype(jnp.bfloat16)
    grad_right = right_block.astype(jnp.bfloat16)

    grad_features = (
        jnp.dot(grad_left, w_left.T, preferred_element_type=jnp.float32)
        + jnp.dot(grad_right, w_right.T, preferred_element_type=jnp.float32)
    ).astype(jnp.bfloat16)
    contract = (((0,), (0,)), ((), ()))
    wleft_part = lax.dot_general(bin_features, grad_left, contract, preferred_element_type=jnp.float32)
    wright_part = lax.dot_general(bin_features, grad_right, contract, preferred_element_type=jnp.float32)
    bit = 1
    while bit < row_count:
        likes = (wleft_part, wright_part, small)
        flat = packed(likes)
        wleft_part, wright_part, small = unpacked(flat + xor_round(flat, "row", row_count, bit), likes)
        bit *= 2

    kernel_sum, point_sum, head_sum = unpacked(small, (kernel_part, point_part, head_part))
    return (
        grad_features,
        grad_scale * wleft_part,
        grad_scale * wright_part,
        grad_scale * kernel_sum,
        grad_scale * point_sum,
        grad_scale * head_sum,
    )


def solution(mesh):
    placed = (P("row", None), P(), P(), P(), P(), P(), P(None, "row", "col"))
    return jax.shard_map(
        body,
        mesh=mesh,
        in_specs=placed,
        out_specs=(P("row", None), P(), P(), P(), P(), P()),
        check_vma=False,
    )
```

```python
import math

import jax
import jax.numpy as jnp
from jax import lax
from jax.sharding import PartitionSpec as P

DILATION_STEP = 4


def silu_slope(values):
    logistic = jax.nn.sigmoid(values)
    return logistic * (1.0 + values * (1.0 - logistic))


def shifted(x, axis, step, count):
    pairs = [(i, i + step) for i in range(count) if 0 <= i + step < count]
    return lax.ppermute(x, axis, pairs)


def packed(parts):
    return jnp.concatenate([p.ravel() for p in parts])


def unpacked(flat, likes):
    out, at = [], 0
    for like in likes:
        out.append(flat[at : at + like.size].reshape(like.shape))
        at += like.size
    return out


def xor_round(flat, axis, count, bit):
    return lax.ppermute(flat, axis, [(i, i ^ bit) for i in range(count)])


def body(bin_features, w_left, w_right, depth_kernel, w_point, w_head, cotangent):
    rows = bin_features.shape[0]
    cols = cotangent.shape[2]
    row_count = lax.axis_size("row")
    col_count = lax.axis_size("col")
    ratio = col_count // row_count
    bins = rows * row_count
    grad_scale = 1.0 / math.sqrt(bins)
    step = DILATION_STEP
    halo = 2 * step
    r = lax.axis_index("row")
    k = lax.axis_index("col")
    part = k % ratio

    left_proj = jnp.dot(bin_features, w_left, preferred_element_type=jnp.float32).astype(jnp.bfloat16)
    right_proj = jnp.dot(bin_features, w_right, preferred_element_type=jnp.float32).astype(jnp.bfloat16)

    tail = (cotangent[:, rows - step :, :], left_proj[rows - halo :], right_proj[rows - halo :])
    head = (cotangent[:, :step, :], left_proj[:halo], right_proj[:halo])
    before = unpacked(shifted(packed(tail), "row", 1, row_count), tail)
    after = unpacked(shifted(packed(head), "row", -1, row_count), head)
    cot_rows = jnp.concatenate([before[0], cotangent, after[0]], axis=1)
    left_ext = jnp.concatenate([before[1], left_proj, after[1]], axis=0)
    right_panel = jnp.concatenate([before[2], right_proj, after[2]], axis=0)
    cot_ext = jnp.concatenate(
        [
            shifted(cot_rows[:, :, cols - step :], "col", 1, col_count),
            cot_rows,
            shifted(cot_rows[:, :, :step], "col", -1, col_count),
        ],
        axis=2,
    )

    def transpose_pairs():
        pairs = []
        for a in range(row_count):
            for b in range(col_count):
                pairs.append((a * col_count + b, (b // ratio) * col_count + ratio * a + b % ratio))
        return pairs

    own_tile = lax.dynamic_slice_in_dim(right_panel, part * cols, cols + 2 * halo, 0)
    right_ext = lax.ppermute(own_tile, ("row", "col"), transpose_pairs())

    row_place = r * rows - halo + lax.broadcasted_iota(jnp.int32, (rows + 2 * halo, 1), 0)
    col_place = k * cols - halo + lax.broadcasted_iota(jnp.int32, (1, cols + 2 * halo), 1)
    valid = (row_place >= 0) & (row_place < bins) & (col_place >= 0) & (col_place < bins)
    pair_sum = right_ext.astype(jnp.float32).T[:, :, None] + left_ext.astype(jnp.float32).T[:, None, :]
    pair_ext = jnp.where(valid.T[None], pair_sum, 0.0).astype(jnp.bfloat16)
    cot_ext = cot_ext.transpose(0, 2, 1)
    cotangent = cotangent.transpose(0, 2, 1)
    taps_by_col = depth_kernel.reshape(3, 3, -1).transpose(1, 0, 2).reshape(depth_kernel.shape)
    depth_kernel = taps_by_col
    rows, cols = cols, rows

    ext_rows = rows + 2 * step
    ext_cols = cols + 2 * step
    conv_ext = jnp.zeros((pair_ext.shape[0], ext_rows, ext_cols), jnp.float32)
    for a in range(3):
        for b in range(3):
            conv_ext = conv_ext + depth_kernel[3 * a + b][:, None, None] * pair_ext[
                :, step * a : step * a + ext_rows, step * b : step * b + ext_cols
            ].astype(jnp.float32)
    conv_tile = conv_ext[:, step : step + rows, step : step + cols]
    hidden_state = jax.nn.silu(conv_tile).astype(jnp.bfloat16)
    mixed_out = jnp.einsum("co,cij->oij", w_point, hidden_state, preferred_element_type=jnp.float32)
    pair_tile = pair_ext[:, halo : halo + rows, halo : halo + cols]
    trunk_matrix = (pair_tile.astype(jnp.float32) + mixed_out).astype(jnp.bfloat16)

    trunk_gradient = (
        grad_scale * jnp.einsum("ch,hij->cij", w_head, cot_ext, preferred_element_type=jnp.float32)
    ).astype(jnp.bfloat16)
    grad_hidden = jnp.einsum("co,oij->cij", w_point, trunk_gradient, preferred_element_type=jnp.float32)
    conv_grad = (grad_hidden * silu_slope(conv_ext)).astype(jnp.bfloat16)
    conv_grad_tile = conv_grad[:, step : step + rows, step : step + cols].astype(jnp.float32)
    trunk_grad_tile = trunk_gradient[:, step : step + rows, step : step + cols]

    backward_pass = trunk_grad_tile.astype(jnp.float32)
    kern_terms = []
    for a in range(3):
        for b in range(3):
            backward_pass = backward_pass + depth_kernel[3 * a + b][:, None, None] * conv_grad[
                :, step * (2 - a) : step * (2 - a) + rows, step * (2 - b) : step * (2 - b) + cols
            ].astype(jnp.float32)
            window = pair_ext[
                :, step + step * a : step + step * a + rows, step + step * b : step + step * b + cols
            ].astype(jnp.float32)
            kern_terms.append(jnp.sum(conv_grad_tile * window, axis=(1, 2)))
    kernel_part = jnp.stack(kern_terms)
    kernel_part = kernel_part.reshape(3, 3, -1).transpose(1, 0, 2).reshape(kernel_part.shape)
    left_part = jnp.sum(backward_pass, axis=1).T
    right_part = jnp.sum(backward_pass, axis=2).T
    rows, cols = cols, rows
    point_part = jnp.einsum(
        "fsk,gsk->fg", hidden_state, trunk_grad_tile, preferred_element_type=jnp.float32
    )
    head_part = jnp.einsum("ydq,gdq->yg", trunk_matrix, cotangent, preferred_element_type=jnp.float32)
    small = packed((kernel_part, point_part, head_part))

    right_moved = lax.ppermute(right_part, ("row", "col"), transpose_pairs())
    bit = ratio
    while bit < col_count:
        likes = (left_part, right_moved, small)
        flat = packed(likes)
        left_part, right_moved, small = unpacked(flat + xor_round(flat, "col", col_count, bit), likes)
        bit *= 2
    right_block = right_moved
    bit = 1
    while bit < ratio:
        likes = (left_part, right_block, small)
        flat = packed(likes)
        got = unpacked(xor_round(flat, "col", col_count, bit), likes)
        left_part = left_part + got[0]
        small = small + got[2]
        upper = (k & bit) != 0
        right_block = jnp.concatenate(
            [jnp.where(upper, got[1], right_block), jnp.where(upper, right_block, got[1])], axis=0
        )
        bit *= 2
    grad_left = left_part.astype(jnp.bfloat16)
    grad_right = right_block.astype(jnp.bfloat16)

    grad_features = (
        jnp.dot(grad_left, w_left.T, preferred_element_type=jnp.float32)
        + jnp.dot(grad_right, w_right.T, preferred_element_type=jnp.float32)
    ).astype(jnp.bfloat16)
    contract = (((0,), (0,)), ((), ()))
    wleft_part = lax.dot_general(bin_features, grad_left, contract, preferred_element_type=jnp.float32)
    wright_part = lax.dot_general(bin_features, grad_right, contract, preferred_element_type=jnp.float32)
    bit = 1
    while bit < row_count:
        likes = (wleft_part, wright_part, small)
        flat = packed(likes)
        wleft_part, wright_part, small = unpacked(flat + xor_round(flat, "row", row_count, bit), likes)
        bit *= 2

    kernel_sum, point_sum, head_sum = unpacked(small, (kernel_part, point_part, head_part))
    return (
        grad_features,
        grad_scale * wleft_part,
        grad_scale * wright_part,
        grad_scale * kernel_sum,
        grad_scale * point_sum,
        grad_scale * head_sum,
    )


def solution(mesh):
    placed = (P("row", None), P(), P(), P(), P(), P(), P(None, "row", "col"))
    return jax.shard_map(
        body,
        mesh=mesh,
        in_specs=placed,
        out_specs=(P("row", None), P(), P(), P(), P(), P()),
        check_vma=False,
    )
```

```python
import math

import jax
import jax.numpy as jnp
from jax import lax
from jax.sharding import PartitionSpec as P

DILATION_STEP = 4


def silu_slope(values):
    logistic = jax.nn.sigmoid(values)
    return logistic * (1.0 + values * (1.0 - logistic))


def shifted(x, axis, step, count):
    pairs = [(i, i + step) for i in range(count) if 0 <= i + step < count]
    return lax.ppermute(x, axis, pairs)


def packed(parts):
    return jnp.concatenate([p.ravel() for p in parts])


def unpacked(flat, likes):
    out, at = [], 0
    for like in likes:
        out.append(flat[at : at + like.size].reshape(like.shape))
        at += like.size
    return out


def xor_round(flat, axis, count, bit):
    return lax.ppermute(flat, axis, [(i, i ^ bit) for i in range(count)])


def body(bin_features, w_left, w_right, depth_kernel, w_point, w_head, cotangent):
    rows = bin_features.shape[0]
    cols = cotangent.shape[2]
    row_count = lax.axis_size("row")
    col_count = lax.axis_size("col")
    ratio = col_count // row_count
    bins = rows * row_count
    grad_scale = 1.0 / math.sqrt(bins)
    step = DILATION_STEP
    halo = 2 * step
    r = lax.axis_index("row")
    k = lax.axis_index("col")
    part = k % ratio

    left_proj = jnp.dot(bin_features, w_left, preferred_element_type=jnp.float32).astype(jnp.bfloat16)
    right_proj = jnp.dot(bin_features, w_right, preferred_element_type=jnp.float32).astype(jnp.bfloat16)

    tail = (cotangent[:, rows - step :, :], left_proj[rows - halo :], right_proj[rows - halo :])
    head = (cotangent[:, :step, :], left_proj[:halo], right_proj[:halo])
    before = unpacked(shifted(packed(tail), "row", 1, row_count), tail)
    after = unpacked(shifted(packed(head), "row", -1, row_count), head)
    cot_rows = jnp.concatenate([before[0], cotangent, after[0]], axis=1)
    left_ext = jnp.concatenate([before[1], left_proj, after[1]], axis=0)
    right_panel = jnp.concatenate([before[2], right_proj, after[2]], axis=0)
    cot_ext = jnp.concatenate(
        [
            shifted(cot_rows[:, :, cols - step :], "col", 1, col_count),
            cot_rows,
            shifted(cot_rows[:, :, :step], "col", -1, col_count),
        ],
        axis=2,
    )

    def transpose_pairs():
        pairs = []
        for a in range(row_count):
            for b in range(col_count):
                pairs.append((a * col_count + b, (b // ratio) * col_count + ratio * a + b % ratio))
        return pairs

    own_tile = lax.dynamic_slice_in_dim(right_panel, part * cols, cols + 2 * halo, 0)
    right_ext = lax.ppermute(own_tile, ("row", "col"), transpose_pairs())

    row_place = r * rows - halo + lax.broadcasted_iota(jnp.int32, (rows + 2 * halo, 1), 0)
    col_place = k * cols - halo + lax.broadcasted_iota(jnp.int32, (1, cols + 2 * halo), 1)
    valid = (row_place >= 0) & (row_place < bins) & (col_place >= 0) & (col_place < bins)
    pair_sum = left_ext.astype(jnp.float32).T[:, :, None] + right_ext.astype(jnp.float32).T[:, None, :]
    pair_ext = jnp.where(valid[None], pair_sum, 0.0).astype(jnp.bfloat16)

    ext_rows = rows + 2 * step
    ext_cols = cols + 2 * step
    conv_ext = jnp.zeros((pair_ext.shape[0], ext_rows, ext_cols), jnp.float32)
    for a in range(3):
        for b in range(3):
            conv_ext = conv_ext + depth_kernel[3 * a + b][:, None, None] * pair_ext[
                :, step * a : step * a + ext_rows, step * b : step * b + ext_cols
            ].astype(jnp.float32)
    conv_tile = conv_ext[:, step : step + rows, step : step + cols]
    hidden_state = jax.nn.silu(conv_tile).astype(jnp.bfloat16)
    mixed_out = jnp.einsum("co,cij->oij", w_point, hidden_state, preferred_element_type=jnp.float32)
    pair_tile = pair_ext[:, halo : halo + rows, halo : halo + cols]
    trunk_matrix = (pair_tile.astype(jnp.float32) + mixed_out).astype(jnp.bfloat16)

    trunk_gradient = (
        grad_scale * jnp.einsum("ch,hij->cij", w_head, cot_ext, preferred_element_type=jnp.float32)
    ).astype(jnp.bfloat16)
    grad_hidden = jnp.einsum("co,oij->cij", w_point, trunk_gradient, preferred_element_type=jnp.float32)
    conv_grad = (grad_hidden * silu_slope(conv_ext)).astype(jnp.bfloat16)
    conv_grad_tile = conv_grad[:, step : step + rows, step : step + cols].astype(jnp.float32)
    trunk_grad_tile = trunk_gradient[:, step : step + rows, step : step + cols]

    backward_pass = trunk_grad_tile.astype(jnp.float32)
    kern_terms = []
    for a in range(3):
        for b in range(3):
            backward_pass = backward_pass + depth_kernel[3 * a + b][:, None, None] * conv_grad[
                :, step * (2 - a) : step * (2 - a) + rows, step * (2 - b) : step * (2 - b) + cols
            ].astype(jnp.float32)
            window = pair_ext[
                :, step + step * a : step + step * a + rows, step + step * b : step + step * b + cols
            ].astype(jnp.float32)
            kern_terms.append(jnp.sum(conv_grad_tile * window, axis=(1, 2)))
    kernel_part = jnp.stack(kern_terms)
    left_part = jnp.sum(backward_pass, axis=2).T
    right_part = jnp.sum(backward_pass, axis=1).T
    point_part = jnp.einsum(
        "fsk,gsk->fg", hidden_state, trunk_grad_tile, preferred_element_type=jnp.float32
    )
    head_part = jnp.einsum("ydq,gdq->yg", trunk_matrix, cotangent, preferred_element_type=jnp.float32)
    small = packed((kernel_part, point_part, head_part))

    right_moved = lax.ppermute(right_part, ("row", "col"), transpose_pairs())
    bit = ratio
    while bit < col_count:
        likes = (left_part, right_moved, small)
        flat = packed(likes)
        left_part, right_moved, small = unpacked(flat + xor_round(flat, "col", col_count, bit), likes)
        bit *= 2
    right_block = right_moved
    bit = 1
    while bit < ratio:
        likes = (left_part, right_block, small)
        flat = packed(likes)
        got = unpacked(xor_round(flat, "col", col_count, bit), likes)
        left_part = left_part + got[0]
        small = small + got[2]
        upper = (k & bit) != 0
        right_block = jnp.concatenate(
            [jnp.where(upper, got[1], right_block), jnp.where(upper, right_block, got[1])], axis=0
        )
        bit *= 2
    grad_left = left_part.astype(jnp.bfloat16)
    grad_right = right_block.astype(jnp.bfloat16)

    grad_features = (
        jnp.dot(grad_left, w_left.T, preferred_element_type=jnp.float32)
        + jnp.dot(grad_right, w_right.T, preferred_element_type=jnp.float32)
    ).astype(jnp.bfloat16)
    contract = (((0,), (0,)), ((), ()))
    wleft_part = lax.dot_general(bin_features, grad_left, contract, preferred_element_type=jnp.float32)
    wright_part = lax.dot_general(bin_features, grad_right, contract, preferred_element_type=jnp.float32)
    bit = 1
    while bit < row_count:
        likes = (wleft_part, wright_part, small)
        flat = packed(likes).astype(jnp.bfloat16)
        got = xor_round(flat, "row", row_count, bit)
        total = flat.astype(jnp.float32) + got.astype(jnp.float32)
        wleft_part, wright_part, small = unpacked(total, likes)
        bit *= 2

    kernel_sum, point_sum, head_sum = unpacked(small, (kernel_part, point_part, head_part))
    return (
        grad_features,
        grad_scale * wleft_part,
        grad_scale * wright_part,
        grad_scale * kernel_sum,
        grad_scale * point_sum,
        grad_scale * head_sum,
    )


def solution(mesh):
    placed = (P("row", None), P(), P(), P(), P(), P(), P(None, "row", "col"))
    return jax.shard_map(
        body,
        mesh=mesh,
        in_specs=placed,
        out_specs=(P("row", None), P(), P(), P(), P(), P()),
        check_vma=False,
    )
```

```python
import math

import jax
import jax.numpy as jnp
from jax import lax
from jax.sharding import PartitionSpec as P

DILATION_STEP = 4


def silu_slope(values):
    logistic = jax.nn.sigmoid(values)
    return logistic * (1.0 + values * (1.0 - logistic))


def shifted(x, axis, step, count):
    pairs = [(i, i + step) for i in range(count) if 0 <= i + step < count]
    return lax.ppermute(x, axis, pairs)


def packed(parts):
    return jnp.concatenate([p.ravel() for p in parts])


def unpacked(flat, likes):
    out, at = [], 0
    for like in likes:
        out.append(flat[at : at + like.size].reshape(like.shape))
        at += like.size
    return out


def xor_round(flat, axis, count, bit):
    return lax.ppermute(flat, axis, [(i, i ^ bit) for i in range(count)])


def body(bin_features, w_left, w_right, depth_kernel, w_point, w_head, cotangent):
    rows = bin_features.shape[0]
    cols = cotangent.shape[2]
    row_count = lax.axis_size("row")
    col_count = lax.axis_size("col")
    ratio = col_count // row_count
    bins = rows * row_count
    grad_scale = 1.0 / math.sqrt(bins)
    step = DILATION_STEP
    halo = 2 * step
    r = lax.axis_index("row")
    k = lax.axis_index("col")
    part = k % ratio

    left_proj = jnp.dot(bin_features, w_left, preferred_element_type=jnp.float32).astype(jnp.bfloat16)
    right_proj = jnp.dot(bin_features, w_right, preferred_element_type=jnp.float32).astype(jnp.bfloat16)

    tail = (cotangent[:, rows - step :, :], left_proj[rows - halo :], right_proj[rows - halo :])
    head = (cotangent[:, :step, :], left_proj[:halo], right_proj[:halo])
    before = unpacked(shifted(packed(tail), "row", 1, row_count), tail)
    after = unpacked(shifted(packed(head), "row", -1, row_count), head)
    cot_rows = jnp.concatenate([before[0], cotangent, after[0]], axis=1)
    left_ext = jnp.concatenate([before[1], left_proj, after[1]], axis=0)
    right_panel = jnp.concatenate([before[2], right_proj, after[2]], axis=0)
    cot_ext = jnp.concatenate(
        [
            shifted(cot_rows[:, :, cols - step :], "col", 1, col_count),
            cot_rows,
            shifted(cot_rows[:, :, :step], "col", -1, col_count),
        ],
        axis=2,
    )

    def transpose_pairs():
        pairs = []
        for a in range(row_count):
            for b in range(col_count):
                pairs.append((a * col_count + b, (b // ratio) * col_count + ratio * a + b % ratio))
        return pairs

    own_tile = lax.dynamic_slice_in_dim(right_panel, part * cols, cols + 2 * halo, 0)
    right_ext = lax.ppermute(own_tile, ("row", "col"), transpose_pairs())

    row_place = r * rows - halo + lax.broadcasted_iota(jnp.int32, (rows + 2 * halo, 1), 0)
    col_place = k * cols - halo + lax.broadcasted_iota(jnp.int32, (1, cols + 2 * halo), 1)
    valid = (row_place >= 0) & (row_place < bins) & (col_place >= 0) & (col_place < bins)
    pair_sum = left_ext.astype(jnp.float32).T[:, :, None] + right_ext.astype(jnp.float32).T[:, None, :]
    pair_ext = jnp.where(valid[None], pair_sum, 0.0).astype(jnp.bfloat16)

    ext_rows = rows + 2 * step
    ext_cols = cols + 2 * step
    conv_ext = jnp.zeros((pair_ext.shape[0], ext_rows, ext_cols), jnp.float32)
    for a in range(3):
        for b in range(3):
            conv_ext = conv_ext + depth_kernel[3 * a + b][:, None, None] * pair_ext[
                :, step * a : step * a + ext_rows, step * b : step * b + ext_cols
            ].astype(jnp.float32)
    conv_tile = conv_ext[:, step : step + rows, step : step + cols]
    hidden_state = jax.nn.silu(conv_tile).astype(jnp.bfloat16)
    mixed_out = jnp.einsum("co,cij->oij", w_point, hidden_state, preferred_element_type=jnp.float32)
    pair_tile = pair_ext[:, halo : halo + rows, halo : halo + cols]
    trunk_matrix = (pair_tile.astype(jnp.float32) + mixed_out).astype(jnp.bfloat16)

    trunk_gradient = (
        grad_scale * jnp.einsum("ch,hij->cij", w_head, cot_ext, preferred_element_type=jnp.float32)
    ).astype(jnp.bfloat16)
    grad_hidden = jnp.einsum("co,oij->cij", w_point, trunk_gradient, preferred_element_type=jnp.float32)
    conv_grad = (grad_hidden * silu_slope(conv_ext)).astype(jnp.bfloat16)
    conv_grad_tile = conv_grad[:, step : step + rows, step : step + cols].astype(jnp.float32)
    trunk_grad_tile = trunk_gradient[:, step : step + rows, step : step + cols]

    backward_pass = trunk_grad_tile.astype(jnp.float32)
    kern_terms = []
    for a in range(3):
        for b in range(3):
            backward_pass = backward_pass + depth_kernel[3 * a + b][:, None, None] * conv_grad[
                :, step * (2 - a) : step * (2 - a) + rows, step * (2 - b) : step * (2 - b) + cols
            ].astype(jnp.float32)
            window = pair_ext[
                :, step + step * a : step + step * a + rows, step + step * b : step + step * b + cols
            ].astype(jnp.float32)
            kern_terms.append(jnp.sum(conv_grad_tile * window, axis=(1, 2)))
    kernel_part = jnp.stack(kern_terms)
    left_part = jnp.sum(backward_pass, axis=2).T
    right_part = jnp.sum(backward_pass, axis=1).T
    point_part = jnp.einsum(
        "fsk,gsk->fg", hidden_state, trunk_grad_tile, preferred_element_type=jnp.float32
    )
    head_part = jnp.einsum("ydq,gdq->yg", trunk_matrix, cotangent, preferred_element_type=jnp.float32)
    small = packed((kernel_part, point_part, head_part))

    right_moved = lax.ppermute(right_part, ("row", "col"), transpose_pairs())
    bit = ratio
    while bit < col_count:
        likes = (left_part, right_moved, small)
        flat = packed(likes).astype(jnp.bfloat16)
        got = xor_round(flat, "col", col_count, bit)
        total = flat.astype(jnp.float32) + got.astype(jnp.float32)
        left_part, right_moved, small = unpacked(total, likes)
        bit *= 2
    right_block = right_moved
    bit = 1
    while bit < ratio:
        likes = (left_part, right_block, small)
        flat = packed(likes).astype(jnp.bfloat16)
        got = unpacked(xor_round(flat, "col", col_count, bit).astype(jnp.float32), likes)
        left_part, right_block, small = unpacked(flat.astype(jnp.float32), likes)
        left_part = left_part + got[0]
        small = small + got[2]
        upper = (k & bit) != 0
        right_block = jnp.concatenate(
            [jnp.where(upper, got[1], right_block), jnp.where(upper, right_block, got[1])], axis=0
        )
        bit *= 2
    grad_left = left_part.astype(jnp.bfloat16)
    grad_right = right_block.astype(jnp.bfloat16)

    grad_features = (
        jnp.dot(grad_left, w_left.T, preferred_element_type=jnp.float32)
        + jnp.dot(grad_right, w_right.T, preferred_element_type=jnp.float32)
    ).astype(jnp.bfloat16)
    contract = (((0,), (0,)), ((), ()))
    wleft_part = lax.dot_general(bin_features, grad_left, contract, preferred_element_type=jnp.float32)
    wright_part = lax.dot_general(bin_features, grad_right, contract, preferred_element_type=jnp.float32)
    bit = 1
    while bit < row_count:
        likes = (wleft_part, wright_part, small)
        flat = packed(likes).astype(jnp.bfloat16)
        got = xor_round(flat, "row", row_count, bit)
        total = flat.astype(jnp.float32) + got.astype(jnp.float32)
        wleft_part, wright_part, small = unpacked(total, likes)
        bit *= 2

    kernel_sum, point_sum, head_sum = unpacked(small, (kernel_part, point_part, head_part))
    return (
        grad_features,
        grad_scale * wleft_part,
        grad_scale * wright_part,
        grad_scale * kernel_sum,
        grad_scale * point_sum,
        grad_scale * head_sum,
    )


def solution(mesh):
    placed = (P("row", None), P(), P(), P(), P(), P(), P(None, "row", "col"))
    return jax.shard_map(
        body,
        mesh=mesh,
        in_specs=placed,
        out_specs=(P("row", None), P(), P(), P(), P(), P()),
        check_vma=False,
    )
```

```python
import math

import jax
import jax.numpy as jnp
from jax import lax
from jax.sharding import PartitionSpec as P

DILATION_STEP = 4


def silu_slope(values):
    logistic = jax.nn.sigmoid(values)
    return logistic * (1.0 + values * (1.0 - logistic))


def shifted(x, axis, step, count):
    pairs = [(i, i + step) for i in range(count) if 0 <= i + step < count]
    return lax.ppermute(x, axis, pairs)


def packed(parts):
    return jnp.concatenate([p.ravel() for p in parts])


def unpacked(flat, likes):
    out, at = [], 0
    for like in likes:
        out.append(flat[at : at + like.size].reshape(like.shape))
        at += like.size
    return out


def xor_round(flat, axis, count, bit):
    return lax.ppermute(flat, axis, [(i, i ^ bit) for i in range(count)])


def body(bin_features, w_left, w_right, depth_kernel, w_point, w_head, cotangent):
    rows = bin_features.shape[0]
    cols = cotangent.shape[2]
    row_count = lax.axis_size("row")
    col_count = lax.axis_size("col")
    ratio = col_count // row_count
    bins = rows * row_count
    grad_scale = 1.0 / math.sqrt(bins)
    step = DILATION_STEP
    halo = 2 * step
    r = lax.axis_index("row")
    k = lax.axis_index("col")
    part = k % ratio

    left_proj = jnp.dot(bin_features, w_left, preferred_element_type=jnp.float32).astype(jnp.bfloat16)
    right_proj = jnp.dot(bin_features, w_right, preferred_element_type=jnp.float32).astype(jnp.bfloat16)

    tail = (cotangent[:, rows - step :, :], left_proj[rows - halo :], right_proj[rows - halo :])
    head = (cotangent[:, :step, :], left_proj[:halo], right_proj[:halo])
    before = unpacked(shifted(packed(tail), "row", 1, row_count), tail)
    after = unpacked(shifted(packed(head), "row", -1, row_count), head)
    cot_rows = jnp.concatenate([before[0], cotangent, after[0]], axis=1)
    left_ext = jnp.concatenate([before[1], left_proj, after[1]], axis=0)
    right_panel = jnp.concatenate([before[2], right_proj, after[2]], axis=0)
    cot_ext = jnp.concatenate(
        [
            shifted(cot_rows[:, :, cols - step :], "col", 1, col_count),
            cot_rows,
            shifted(cot_rows[:, :, :step], "col", -1, col_count),
        ],
        axis=2,
    )

    def transpose_pairs():
        pairs = []
        for a in range(row_count):
            for b in range(col_count):
                pairs.append((a * col_count + b, (b // ratio) * col_count + ratio * a + b % ratio))
        return pairs

    own_tile = lax.dynamic_slice_in_dim(right_panel, part * cols, cols + 2 * halo, 0)
    right_ext = lax.ppermute(own_tile, ("row", "col"), transpose_pairs())

    row_place = r * rows - halo + lax.broadcasted_iota(jnp.int32, (rows + 2 * halo, 1), 0)
    col_place = k * cols - halo + lax.broadcasted_iota(jnp.int32, (1, cols + 2 * halo), 1)
    valid = (row_place >= 0) & (row_place < bins) & (col_place >= 0) & (col_place < bins)
    pair_sum = left_ext.astype(jnp.float32).T[:, :, None] + right_ext.astype(jnp.float32).T[:, None, :]
    pair_ext = jnp.where(valid[None], pair_sum, 0.0).astype(jnp.bfloat16)

    ext_rows = rows + 2 * step
    ext_cols = cols + 2 * step
    conv_ext = jnp.zeros((pair_ext.shape[0], ext_rows, ext_cols), jnp.float32)
    for a in range(3):
        for b in range(3):
            conv_ext = conv_ext + depth_kernel[3 * a + b][:, None, None] * pair_ext[
                :, step * a : step * a + ext_rows, step * b : step * b + ext_cols
            ].astype(jnp.float32)
    conv_tile = conv_ext[:, step : step + rows, step : step + cols]
    hidden_state = jax.nn.silu(conv_tile).astype(jnp.bfloat16)
    mixed_out = jnp.einsum("co,cij->oij", w_point, hidden_state, preferred_element_type=jnp.float32)
    pair_tile = pair_ext[:, halo : halo + rows, halo : halo + cols]
    trunk_matrix = (pair_tile.astype(jnp.float32) + mixed_out).astype(jnp.bfloat16)

    trunk_gradient = (
        grad_scale * jnp.einsum("ch,hij->cij", w_head, cot_ext, preferred_element_type=jnp.float32)
    ).astype(jnp.bfloat16)
    grad_hidden = jnp.einsum("co,oij->cij", w_point, trunk_gradient, preferred_element_type=jnp.float32)
    conv_grad = (grad_hidden * silu_slope(conv_ext)).astype(jnp.bfloat16)
    conv_grad_tile = conv_grad[:, step : step + rows, step : step + cols].astype(jnp.float32)
    trunk_grad_tile = trunk_gradient[:, step : step + rows, step : step + cols]

    backward_pass = trunk_grad_tile.astype(jnp.float32)
    kern_terms = []
    for a in range(3):
        for b in range(3):
            backward_pass = backward_pass + depth_kernel[3 * a + b][:, None, None] * conv_grad[
                :, step * (2 - a) : step * (2 - a) + rows, step * (2 - b) : step * (2 - b) + cols
            ].astype(jnp.float32)
            window = pair_ext[
                :, step + step * a : step + step * a + rows, step + step * b : step + step * b + cols
            ].astype(jnp.float32)
            kern_terms.append(jnp.sum(conv_grad_tile * window, axis=(1, 2)))
    kernel_part = jnp.stack(kern_terms)
    left_part = jnp.sum(backward_pass, axis=2).T
    right_part = jnp.sum(backward_pass, axis=1).T
    point_part = jnp.einsum(
        "fsk,gsk->fg", hidden_state, trunk_grad_tile, preferred_element_type=jnp.float32
    )
    head_part = jnp.einsum("ydq,gdq->yg", trunk_matrix, cotangent, preferred_element_type=jnp.float32)
    small = packed((kernel_part, point_part, head_part))

    right_moved = lax.ppermute(right_part, ("row", "col"), transpose_pairs())
    bit = ratio
    while bit < col_count:
        likes = (left_part, right_moved, small)
        flat = packed(likes).astype(jnp.bfloat16)
        got = xor_round(flat, "col", col_count, bit)
        total = flat.astype(jnp.float32) + got.astype(jnp.float32)
        left_part, right_moved, small = unpacked(total, likes)
        bit *= 2
    right_block = right_moved
    bit = 1
    while bit < ratio:
        likes = (left_part, right_block, small)
        flat = packed(likes).astype(jnp.bfloat16)
        got = unpacked(xor_round(flat, "col", col_count, bit).astype(jnp.float32), likes)
        left_part, right_block, small = unpacked(flat.astype(jnp.float32), likes)
        left_part = left_part + got[0]
        small = small + got[2]
        upper = (k & bit) != 0
        right_block = jnp.concatenate(
            [jnp.where(upper, got[1], right_block), jnp.where(upper, right_block, got[1])], axis=0
        )
        bit *= 2
    grad_left = left_part.astype(jnp.bfloat16)
    grad_right = right_block.astype(jnp.bfloat16)

    grad_features = (
        jnp.dot(grad_left, w_left.T, preferred_element_type=jnp.float32)
        + jnp.dot(grad_right, w_right.T, preferred_element_type=jnp.float32)
    ).astype(jnp.bfloat16)
    contract = (((0,), (0,)), ((), ()))
    wleft_part = lax.dot_general(bin_features, grad_left, contract, preferred_element_type=jnp.float32)
    wright_part = lax.dot_general(bin_features, grad_right, contract, preferred_element_type=jnp.float32)
    wleft_part, wright_part, small = (grad_scale * wleft_part, grad_scale * wright_part, grad_scale * small)
    bit = 1
    while bit < row_count:
        likes = (wleft_part, wright_part, small)
        flat = packed(likes).astype(jnp.bfloat16)
        got = xor_round(flat, "row", row_count, bit)
        total = flat.astype(jnp.float32) + got.astype(jnp.float32)
        wleft_part, wright_part, small = unpacked(total, likes)
        bit *= 2

    kernel_sum, point_sum, head_sum = unpacked(small, (kernel_part, point_part, head_part))
    return (grad_features, wleft_part, wright_part, kernel_sum, point_sum, head_sum)


def solution(mesh):
    placed = (P("row", None), P(), P(), P(), P(), P(), P(None, "row", "col"))
    return jax.shard_map(
        body,
        mesh=mesh,
        in_specs=placed,
        out_specs=(P("row", None), P(), P(), P(), P(), P()),
        check_vma=False,
    )
```

```python
import math

import jax
import jax.numpy as jnp
from jax import lax
from jax.sharding import PartitionSpec as P

DILATION_STEP = 4


def silu_slope(values):
    logistic = jax.nn.sigmoid(values)
    return logistic * (1.0 + values * (1.0 - logistic))


def shifted(x, axis, step, count):
    pairs = [(i, i + step) for i in range(count) if 0 <= i + step < count]
    return lax.ppermute(x, axis, pairs)


def packed(parts):
    return jnp.concatenate([p.ravel() for p in parts])


def unpacked(flat, likes):
    out, at = [], 0
    for like in likes:
        out.append(flat[at : at + like.size].reshape(like.shape))
        at += like.size
    return out


def xor_round(flat, axis, count, bit):
    return lax.ppermute(flat, axis, [(i, i ^ bit) for i in range(count)])


def body(bin_features, w_left, w_right, depth_kernel, w_point, w_head, cotangent):
    rows = bin_features.shape[0]
    cols = cotangent.shape[2]
    row_count = lax.axis_size("row")
    col_count = lax.axis_size("col")
    ratio = col_count // row_count
    bins = rows * row_count
    grad_scale = 1.0 / math.sqrt(bins)
    step = DILATION_STEP
    halo = 2 * step
    r = lax.axis_index("row")
    k = lax.axis_index("col")
    part = k % ratio

    left_proj = jnp.dot(bin_features, w_left, preferred_element_type=jnp.float32).astype(jnp.bfloat16)
    right_proj = jnp.dot(bin_features, w_right, preferred_element_type=jnp.float32).astype(jnp.bfloat16)

    tail = (cotangent[:, rows - step :, :], left_proj[rows - halo :], right_proj[rows - halo :])
    head = (cotangent[:, :step, :], left_proj[:halo], right_proj[:halo])
    before = unpacked(shifted(packed(tail), "row", 1, row_count), tail)
    after = unpacked(shifted(packed(head), "row", -1, row_count), head)
    cot_rows = jnp.concatenate([before[0], cotangent, after[0]], axis=1)
    left_ext = jnp.concatenate([before[1], left_proj, after[1]], axis=0)
    right_panel = jnp.concatenate([before[2], right_proj, after[2]], axis=0)

    def transpose_pairs():
        pairs = []
        for a in range(row_count):
            for b in range(col_count):
                pairs.append((a * col_count + b, (b // ratio) * col_count + ratio * a + b % ratio))
        return pairs

    own_tile = lax.dynamic_slice_in_dim(right_panel, part * cols, cols + 2 * halo, 0)
    right_ext = lax.ppermute(own_tile, ("row", "col"), transpose_pairs())

    row_place = r * rows - halo + lax.broadcasted_iota(jnp.int32, (rows + 2 * halo, 1), 0)
    col_place = k * cols - halo + lax.broadcasted_iota(jnp.int32, (1, cols + 2 * halo), 1)
    valid = (row_place >= 0) & (row_place < bins) & (col_place >= 0) & (col_place < bins)
    pair_sum = left_ext.astype(jnp.float32).T[:, :, None] + right_ext.astype(jnp.float32).T[:, None, :]
    pair_ext = jnp.where(valid[None], pair_sum, 0.0).astype(jnp.bfloat16)

    ext_rows = rows + 2 * step
    ext_cols = cols + 2 * step
    conv_ext = jnp.zeros((pair_ext.shape[0], ext_rows, ext_cols), jnp.float32)
    for a in range(3):
        for b in range(3):
            conv_ext = conv_ext + depth_kernel[3 * a + b][:, None, None] * pair_ext[
                :, step * a : step * a + ext_rows, step * b : step * b + ext_cols
            ].astype(jnp.float32)
    left_strip, right_strip, conv_ext = lax.optimization_barrier(
        (cot_rows[:, :, cols - step :], cot_rows[:, :, :step], conv_ext)
    )
    cot_ext = jnp.concatenate(
        [shifted(left_strip, "col", 1, col_count), cot_rows, shifted(right_strip, "col", -1, col_count)],
        axis=2,
    )
    conv_tile = conv_ext[:, step : step + rows, step : step + cols]
    hidden_state = jax.nn.silu(conv_tile).astype(jnp.bfloat16)
    mixed_out = jnp.einsum("co,cij->oij", w_point, hidden_state, preferred_element_type=jnp.float32)
    pair_tile = pair_ext[:, halo : halo + rows, halo : halo + cols]
    trunk_matrix = (pair_tile.astype(jnp.float32) + mixed_out).astype(jnp.bfloat16)

    trunk_gradient = (
        grad_scale * jnp.einsum("ch,hij->cij", w_head, cot_ext, preferred_element_type=jnp.float32)
    ).astype(jnp.bfloat16)
    grad_hidden = jnp.einsum("co,oij->cij", w_point, trunk_gradient, preferred_element_type=jnp.float32)
    conv_grad = (grad_hidden * silu_slope(conv_ext)).astype(jnp.bfloat16)
    conv_grad_tile = conv_grad[:, step : step + rows, step : step + cols].astype(jnp.float32)
    trunk_grad_tile = trunk_gradient[:, step : step + rows, step : step + cols]

    backward_pass = trunk_grad_tile.astype(jnp.float32)
    kern_terms = []
    for a in range(3):
        for b in range(3):
            backward_pass = backward_pass + depth_kernel[3 * a + b][:, None, None] * conv_grad[
                :, step * (2 - a) : step * (2 - a) + rows, step * (2 - b) : step * (2 - b) + cols
            ].astype(jnp.float32)
            window = pair_ext[
                :, step + step * a : step + step * a + rows, step + step * b : step + step * b + cols
            ].astype(jnp.float32)
            kern_terms.append(jnp.sum(conv_grad_tile * window, axis=(1, 2)))
    kernel_part = jnp.stack(kern_terms)
    left_part = jnp.sum(backward_pass, axis=2).T
    right_part = jnp.sum(backward_pass, axis=1).T
    point_part = jnp.einsum(
        "fsk,gsk->fg", hidden_state, trunk_grad_tile, preferred_element_type=jnp.float32
    )
    head_part = jnp.einsum("ydq,gdq->yg", trunk_matrix, cotangent, preferred_element_type=jnp.float32)
    small = packed((kernel_part, point_part, head_part))

    right_moved = lax.ppermute(right_part, ("row", "col"), transpose_pairs())
    bit = ratio
    while bit < col_count:
        likes = (left_part, right_moved, small)
        flat = packed(likes).astype(jnp.bfloat16)
        got = xor_round(flat, "col", col_count, bit)
        total = flat.astype(jnp.float32) + got.astype(jnp.float32)
        left_part, right_moved, small = unpacked(total, likes)
        bit *= 2
    right_block = right_moved
    bit = 1
    while bit < ratio:
        likes = (left_part, right_block, small)
        flat = packed(likes).astype(jnp.bfloat16)
        got = unpacked(xor_round(flat, "col", col_count, bit).astype(jnp.float32), likes)
        left_part, right_block, small = unpacked(flat.astype(jnp.float32), likes)
        left_part = left_part + got[0]
        small = small + got[2]
        upper = (k & bit) != 0
        right_block = jnp.concatenate(
            [jnp.where(upper, got[1], right_block), jnp.where(upper, right_block, got[1])], axis=0
        )
        bit *= 2
    grad_left = left_part.astype(jnp.bfloat16)
    grad_right = right_block.astype(jnp.bfloat16)

    grad_features = (
        jnp.dot(grad_left, w_left.T, preferred_element_type=jnp.float32)
        + jnp.dot(grad_right, w_right.T, preferred_element_type=jnp.float32)
    ).astype(jnp.bfloat16)
    contract = (((0,), (0,)), ((), ()))
    wleft_part = lax.dot_general(bin_features, grad_left, contract, preferred_element_type=jnp.float32)
    wright_part = lax.dot_general(bin_features, grad_right, contract, preferred_element_type=jnp.float32)
    bit = 1
    while bit < row_count:
        likes = (wleft_part, wright_part, small)
        flat = packed(likes).astype(jnp.bfloat16)
        got = xor_round(flat, "row", row_count, bit)
        total = flat.astype(jnp.float32) + got.astype(jnp.float32)
        wleft_part, wright_part, small = unpacked(total, likes)
        bit *= 2

    kernel_sum, point_sum, head_sum = unpacked(small, (kernel_part, point_part, head_part))
    return (
        grad_features,
        grad_scale * wleft_part,
        grad_scale * wright_part,
        grad_scale * kernel_sum,
        grad_scale * point_sum,
        grad_scale * head_sum,
    )


def solution(mesh):
    placed = (P("row", None), P(), P(), P(), P(), P(), P(None, "row", "col"))
    return jax.shard_map(
        body,
        mesh=mesh,
        in_specs=placed,
        out_specs=(P("row", None), P(), P(), P(), P(), P()),
        check_vma=False,
    )
```

```python
import math

import jax
import jax.numpy as jnp
from jax import lax
from jax.sharding import PartitionSpec as P

DILATION_STEP = 4


def silu_slope(values):
    logistic = jax.nn.sigmoid(values)
    return logistic * (1.0 + values * (1.0 - logistic))


def shifted(x, axis, step, count):
    pairs = [(i, i + step) for i in range(count) if 0 <= i + step < count]
    return lax.ppermute(x, axis, pairs)


def packed(parts):
    return jnp.concatenate([p.ravel() for p in parts])


def unpacked(flat, likes):
    out, at = [], 0
    for like in likes:
        out.append(flat[at : at + like.size].reshape(like.shape))
        at += like.size
    return out


def xor_round(flat, axis, count, bit):
    return lax.ppermute(flat, axis, [(i, i ^ bit) for i in range(count)])


def body(bin_features, w_left, w_right, depth_kernel, w_point, w_head, cotangent):
    rows = bin_features.shape[0]
    cols = cotangent.shape[2]
    row_count = lax.axis_size("row")
    col_count = lax.axis_size("col")
    ratio = col_count // row_count
    bins = rows * row_count
    grad_scale = 1.0 / math.sqrt(bins)
    step = DILATION_STEP
    halo = 2 * step
    r = lax.axis_index("row")
    k = lax.axis_index("col")
    part = k % ratio

    left_proj = jnp.dot(bin_features, w_left, preferred_element_type=jnp.float32).astype(jnp.bfloat16)
    right_proj = jnp.dot(bin_features, w_right, preferred_element_type=jnp.float32).astype(jnp.bfloat16)

    tail = (cotangent[:, rows - step :, :], left_proj[rows - halo :])
    head = (cotangent[:, :step, :], left_proj[:halo])
    before = unpacked(shifted(packed(tail), "row", 1, row_count), tail)
    after = unpacked(shifted(packed(head), "row", -1, row_count), head)
    cot_rows = jnp.concatenate([before[0], cotangent, after[0]], axis=1)
    left_ext = jnp.concatenate([before[1], left_proj, after[1]], axis=0)

    def transpose_pairs(shift=0):
        pairs = []
        for a in range(row_count):
            for b in range(col_count):
                tile = ratio * a + b % ratio + shift
                if 0 <= tile < col_count:
                    pairs.append((a * col_count + b, (b // ratio) * col_count + tile))
        return pairs

    own_tile = lax.dynamic_slice_in_dim(right_proj, part * cols, cols, 0)
    right_ext = jnp.concatenate(
        [
            lax.ppermute(own_tile[cols - halo :], ("row", "col"), transpose_pairs(1)),
            lax.ppermute(own_tile, ("row", "col"), transpose_pairs()),
            lax.ppermute(own_tile[:halo], ("row", "col"), transpose_pairs(-1)),
        ],
        axis=0,
    )

    row_place = r * rows - halo + lax.broadcasted_iota(jnp.int32, (rows + 2 * halo, 1), 0)
    col_place = k * cols - halo + lax.broadcasted_iota(jnp.int32, (1, cols + 2 * halo), 1)
    valid = (row_place >= 0) & (row_place < bins) & (col_place >= 0) & (col_place < bins)
    pair_sum = left_ext.astype(jnp.float32).T[:, :, None] + right_ext.astype(jnp.float32).T[:, None, :]
    pair_ext = jnp.where(valid[None], pair_sum, 0.0).astype(jnp.bfloat16)

    ext_rows = rows + 2 * step
    ext_cols = cols + 2 * step
    conv_ext = jnp.zeros((pair_ext.shape[0], ext_rows, ext_cols), jnp.float32)
    for a in range(3):
        for b in range(3):
            conv_ext = conv_ext + depth_kernel[3 * a + b][:, None, None] * pair_ext[
                :, step * a : step * a + ext_rows, step * b : step * b + ext_cols
            ].astype(jnp.float32)
    left_strip, right_strip, conv_ext = lax.optimization_barrier(
        (cot_rows[:, :, cols - step :], cot_rows[:, :, :step], conv_ext)
    )
    cot_ext = jnp.concatenate(
        [shifted(left_strip, "col", 1, col_count), cot_rows, shifted(right_strip, "col", -1, col_count)],
        axis=2,
    )
    conv_tile = conv_ext[:, step : step + rows, step : step + cols]
    hidden_state = jax.nn.silu(conv_tile).astype(jnp.bfloat16)
    mixed_out = jnp.einsum("co,cij->oij", w_point, hidden_state, preferred_element_type=jnp.float32)
    pair_tile = pair_ext[:, halo : halo + rows, halo : halo + cols]
    trunk_matrix = (pair_tile.astype(jnp.float32) + mixed_out).astype(jnp.bfloat16)

    trunk_gradient = (
        grad_scale * jnp.einsum("ch,hij->cij", w_head, cot_ext, preferred_element_type=jnp.float32)
    ).astype(jnp.bfloat16)
    grad_hidden = jnp.einsum("co,oij->cij", w_point, trunk_gradient, preferred_element_type=jnp.float32)
    conv_grad = (grad_hidden * silu_slope(conv_ext)).astype(jnp.bfloat16)
    conv_grad_tile = conv_grad[:, step : step + rows, step : step + cols].astype(jnp.float32)
    trunk_grad_tile = trunk_gradient[:, step : step + rows, step : step + cols]

    backward_pass = trunk_grad_tile.astype(jnp.float32)
    kern_terms = []
    for a in range(3):
        for b in range(3):
            backward_pass = backward_pass + depth_kernel[3 * a + b][:, None, None] * conv_grad[
                :, step * (2 - a) : step * (2 - a) + rows, step * (2 - b) : step * (2 - b) + cols
            ].astype(jnp.float32)
            window = pair_ext[
                :, step + step * a : step + step * a + rows, step + step * b : step + step * b + cols
            ].astype(jnp.float32)
            kern_terms.append(jnp.sum(conv_grad_tile * window, axis=(1, 2)))
    kernel_part = jnp.stack(kern_terms)
    left_part = jnp.sum(backward_pass, axis=2).T
    right_part = jnp.sum(backward_pass, axis=1).T
    point_part = jnp.einsum(
        "fsk,gsk->fg", hidden_state, trunk_grad_tile, preferred_element_type=jnp.float32
    )
    head_part = jnp.einsum("ydq,gdq->yg", trunk_matrix, cotangent, preferred_element_type=jnp.float32)
    small = packed((kernel_part, point_part, head_part))

    right_moved = lax.ppermute(right_part, ("row", "col"), transpose_pairs())
    bit = ratio
    while bit < col_count:
        likes = (left_part, right_moved, small)
        flat = packed(likes).astype(jnp.bfloat16)
        got = xor_round(flat, "col", col_count, bit)
        total = flat.astype(jnp.float32) + got.astype(jnp.float32)
        left_part, right_moved, small = unpacked(total, likes)
        bit *= 2
    right_block = right_moved
    bit = 1
    while bit < ratio:
        likes = (left_part, right_block, small)
        flat = packed(likes).astype(jnp.bfloat16)
        got = unpacked(xor_round(flat, "col", col_count, bit).astype(jnp.float32), likes)
        left_part, right_block, small = unpacked(flat.astype(jnp.float32), likes)
        left_part = left_part + got[0]
        small = small + got[2]
        upper = (k & bit) != 0
        right_block = jnp.concatenate(
            [jnp.where(upper, got[1], right_block), jnp.where(upper, right_block, got[1])], axis=0
        )
        bit *= 2
    grad_left = left_part.astype(jnp.bfloat16)
    grad_right = right_block.astype(jnp.bfloat16)

    grad_features = (
        jnp.dot(grad_left, w_left.T, preferred_element_type=jnp.float32)
        + jnp.dot(grad_right, w_right.T, preferred_element_type=jnp.float32)
    ).astype(jnp.bfloat16)
    contract = (((0,), (0,)), ((), ()))
    wleft_part = lax.dot_general(bin_features, grad_left, contract, preferred_element_type=jnp.float32)
    wright_part = lax.dot_general(bin_features, grad_right, contract, preferred_element_type=jnp.float32)
    bit = 1
    while bit < row_count:
        likes = (wleft_part, wright_part, small)
        flat = packed(likes).astype(jnp.bfloat16)
        got = xor_round(flat, "row", row_count, bit)
        total = flat.astype(jnp.float32) + got.astype(jnp.float32)
        wleft_part, wright_part, small = unpacked(total, likes)
        bit *= 2

    kernel_sum, point_sum, head_sum = unpacked(small, (kernel_part, point_part, head_part))
    return (
        grad_features,
        grad_scale * wleft_part,
        grad_scale * wright_part,
        grad_scale * kernel_sum,
        grad_scale * point_sum,
        grad_scale * head_sum,
    )


def solution(mesh):
    placed = (P("row", None), P(), P(), P(), P(), P(), P(None, "row", "col"))
    return jax.shard_map(
        body,
        mesh=mesh,
        in_specs=placed,
        out_specs=(P("row", None), P(), P(), P(), P(), P()),
        check_vma=False,
    )
```

```python
import math

import jax
import jax.numpy as jnp
from jax import lax
from jax.sharding import PartitionSpec as P

DILATION_STEP = 4


def silu_slope(values):
    logistic = jax.nn.sigmoid(values)
    return logistic * (1.0 + values * (1.0 - logistic))


def shifted(x, axis, step, count):
    pairs = [(i, i + step) for i in range(count) if 0 <= i + step < count]
    return lax.ppermute(x, axis, pairs)


def packed(parts):
    return jnp.concatenate([p.ravel() for p in parts])


def unpacked(flat, likes):
    out, at = [], 0
    for like in likes:
        out.append(flat[at : at + like.size].reshape(like.shape))
        at += like.size
    return out


def xor_round(flat, axis, count, bit):
    return lax.ppermute(flat, axis, [(i, i ^ bit) for i in range(count)])


def body(bin_features, w_left, w_right, depth_kernel, w_point, w_head, cotangent):
    rows = bin_features.shape[0]
    cols = cotangent.shape[2]
    row_count = lax.axis_size("row")
    col_count = lax.axis_size("col")
    ratio = col_count // row_count
    bins = rows * row_count
    grad_scale = 1.0 / math.sqrt(bins)
    step = DILATION_STEP
    halo = 2 * step
    r = lax.axis_index("row")
    k = lax.axis_index("col")
    part = k % ratio

    left_proj = jnp.dot(bin_features, w_left, preferred_element_type=jnp.float32).astype(jnp.bfloat16)
    right_proj = jnp.dot(bin_features, w_right, preferred_element_type=jnp.float32).astype(jnp.bfloat16)

    tail = (cotangent[:, rows - step :, :], left_proj[rows - halo :], right_proj[rows - halo :])
    head = (cotangent[:, :step, :], left_proj[:halo], right_proj[:halo])
    before = unpacked(shifted(packed(tail), "row", 1, row_count), tail)
    after = unpacked(shifted(packed(head), "row", -1, row_count), head)
    cot_rows = jnp.concatenate([before[0], cotangent, after[0]], axis=1)
    left_ext = jnp.concatenate([before[1], left_proj, after[1]], axis=0)
    right_panel = jnp.concatenate([before[2], right_proj, after[2]], axis=0)
    cot_ext = jnp.concatenate(
        [
            shifted(cot_rows[:, :, cols - step :], "col", 1, col_count),
            cot_rows,
            shifted(cot_rows[:, :, :step], "col", -1, col_count),
        ],
        axis=2,
    )

    def transpose_pairs():
        pairs = []
        for a in range(row_count):
            for b in range(col_count):
                pairs.append((a * col_count + b, (b // ratio) * col_count + ratio * a + b % ratio))
        return pairs

    own_tile = lax.dynamic_slice_in_dim(right_panel, part * cols, cols + 2 * halo, 0)
    right_ext = lax.ppermute(own_tile, ("row", "col"), transpose_pairs())

    row_place = r * rows - halo + lax.broadcasted_iota(jnp.int32, (rows + 2 * halo, 1), 0)
    col_place = k * cols - halo + lax.broadcasted_iota(jnp.int32, (1, cols + 2 * halo), 1)
    valid = (row_place >= 0) & (row_place < bins) & (col_place >= 0) & (col_place < bins)
    pair_sum = left_ext.astype(jnp.float32).T[:, :, None] + right_ext.astype(jnp.float32).T[:, None, :]
    pair_ext = jnp.where(valid[None], pair_sum, 0.0).astype(jnp.bfloat16)

    ext_rows = rows + 2 * step
    ext_cols = cols + 2 * step
    conv_ext = jnp.zeros((pair_ext.shape[0], ext_rows, ext_cols), jnp.float32)
    for a in range(3):
        for b in range(3):
            conv_ext = conv_ext + depth_kernel[3 * a + b][:, None, None] * pair_ext[
                :, step * a : step * a + ext_rows, step * b : step * b + ext_cols
            ].astype(jnp.float32)
    conv_tile = conv_ext[:, step : step + rows, step : step + cols]
    hidden_state = jax.nn.silu(conv_tile).astype(jnp.bfloat16)
    mixed_out = jnp.einsum("co,cij->oij", w_point, hidden_state, preferred_element_type=jnp.float32)
    pair_tile = pair_ext[:, halo : halo + rows, halo : halo + cols]
    trunk_matrix = (pair_tile.astype(jnp.float32) + mixed_out).astype(jnp.bfloat16)

    trunk_gradient = (
        grad_scale * jnp.einsum("ch,hij->cij", w_head, cot_ext, preferred_element_type=jnp.float32)
    ).astype(jnp.bfloat16)
    grad_hidden = jnp.einsum("co,oij->cij", w_point, trunk_gradient, preferred_element_type=jnp.float32)
    conv_grad = (grad_hidden * silu_slope(conv_ext)).astype(jnp.bfloat16)
    conv_grad_tile = conv_grad[:, step : step + rows, step : step + cols].astype(jnp.float32)
    trunk_grad_tile = trunk_gradient[:, step : step + rows, step : step + cols]

    backward_pass = trunk_grad_tile.astype(jnp.float32)
    kern_terms = []
    for a in range(3):
        for b in range(3):
            backward_pass = backward_pass + depth_kernel[3 * a + b][:, None, None] * conv_grad[
                :, step * (2 - a) : step * (2 - a) + rows, step * (2 - b) : step * (2 - b) + cols
            ].astype(jnp.float32)
            window = pair_ext[
                :, step + step * a : step + step * a + rows, step + step * b : step + step * b + cols
            ].astype(jnp.float32)
            kern_terms.append(jnp.sum(conv_grad_tile * window, axis=(1, 2)))
    kernel_part = jnp.stack(kern_terms)
    left_part = jnp.sum(backward_pass, axis=2).T
    right_part = jnp.sum(backward_pass, axis=1).T
    point_part = jnp.einsum(
        "fsk,gsk->fg", hidden_state, trunk_grad_tile, preferred_element_type=jnp.float32
    )
    head_part = jnp.einsum("ydq,gdq->yg", trunk_matrix, cotangent, preferred_element_type=jnp.float32)
    small = packed((kernel_part, point_part, head_part))

    right_moved = lax.ppermute(right_part, ("row", "col"), transpose_pairs())
    bit = col_count // 2
    while bit >= ratio:
        likes = (left_part, right_moved, small)
        flat = packed(likes).astype(jnp.bfloat16)
        got = xor_round(flat, "col", col_count, bit)
        total = flat.astype(jnp.float32) + got.astype(jnp.float32)
        left_part, right_moved, small = unpacked(total, likes)
        bit //= 2
    right_block = right_moved
    bit = 1
    while bit < ratio:
        likes = (left_part, right_block, small)
        flat = packed(likes).astype(jnp.bfloat16)
        got = unpacked(xor_round(flat, "col", col_count, bit).astype(jnp.float32), likes)
        left_part, right_block, small = unpacked(flat.astype(jnp.float32), likes)
        left_part = left_part + got[0]
        small = small + got[2]
        upper = (k & bit) != 0
        right_block = jnp.concatenate(
            [jnp.where(upper, got[1], right_block), jnp.where(upper, right_block, got[1])], axis=0
        )
        bit *= 2
    grad_left = left_part.astype(jnp.bfloat16)
    grad_right = right_block.astype(jnp.bfloat16)

    grad_features = (
        jnp.dot(grad_left, w_left.T, preferred_element_type=jnp.float32)
        + jnp.dot(grad_right, w_right.T, preferred_element_type=jnp.float32)
    ).astype(jnp.bfloat16)
    contract = (((0,), (0,)), ((), ()))
    wleft_part = lax.dot_general(bin_features, grad_left, contract, preferred_element_type=jnp.float32)
    wright_part = lax.dot_general(bin_features, grad_right, contract, preferred_element_type=jnp.float32)
    bit = row_count // 2
    while bit >= 1:
        likes = (wleft_part, wright_part, small)
        flat = packed(likes).astype(jnp.bfloat16)
        got = xor_round(flat, "row", row_count, bit)
        total = flat.astype(jnp.float32) + got.astype(jnp.float32)
        wleft_part, wright_part, small = unpacked(total, likes)
        bit //= 2

    kernel_sum, point_sum, head_sum = unpacked(small, (kernel_part, point_part, head_part))
    return (
        grad_features,
        grad_scale * wleft_part,
        grad_scale * wright_part,
        grad_scale * kernel_sum,
        grad_scale * point_sum,
        grad_scale * head_sum,
    )


def solution(mesh):
    placed = (P("row", None), P(), P(), P(), P(), P(), P(None, "row", "col"))
    return jax.shard_map(
        body,
        mesh=mesh,
        in_specs=placed,
        out_specs=(P("row", None), P(), P(), P(), P(), P()),
        check_vma=False,
    )
```

```python
import math

import jax
import jax.numpy as jnp
from jax import lax
from jax.sharding import PartitionSpec as P

DILATION_STEP = 4


def silu_slope(values):
    logistic = jax.nn.sigmoid(values)
    return logistic * (1.0 + values * (1.0 - logistic))


def shifted(x, axis, step, count):
    pairs = [(i, i + step) for i in range(count) if 0 <= i + step < count]
    return lax.ppermute(x, axis, pairs)


def packed(parts):
    return jnp.concatenate([p.ravel() for p in parts])


def unpacked(flat, likes):
    out, at = [], 0
    for like in likes:
        out.append(flat[at : at + like.size].reshape(like.shape))
        at += like.size
    return out


def xor_round(flat, axis, count, bit):
    return lax.ppermute(flat, axis, [(i, i ^ bit) for i in range(count)])


def body(bin_features, w_left, w_right, depth_kernel, w_point, w_head, cotangent):
    rows = bin_features.shape[0]
    cols = cotangent.shape[2]
    row_count = lax.axis_size("row")
    col_count = lax.axis_size("col")
    ratio = col_count // row_count
    bins = rows * row_count
    grad_scale = 1.0 / math.sqrt(bins)
    step = DILATION_STEP
    halo = 2 * step
    r = lax.axis_index("row")
    k = lax.axis_index("col")
    part = k % ratio

    left_proj = jnp.dot(bin_features, w_left, preferred_element_type=jnp.float32).astype(jnp.bfloat16)
    right_proj = jnp.dot(bin_features, w_right, preferred_element_type=jnp.float32).astype(jnp.bfloat16)

    tail = (cotangent[:, rows - step :, :], left_proj[rows - halo :], right_proj[rows - halo :])
    head = (cotangent[:, :step, :], left_proj[:halo], right_proj[:halo])
    before = unpacked(shifted(packed(tail), "row", 1, row_count), tail)
    after = unpacked(shifted(packed(head), "row", -1, row_count), head)
    cot_rows = jnp.concatenate([before[0], cotangent, after[0]], axis=1)
    left_ext = jnp.concatenate([before[1], left_proj, after[1]], axis=0)
    right_panel = jnp.concatenate([before[2], right_proj, after[2]], axis=0)
    cot_ext = jnp.concatenate(
        [
            shifted(cot_rows[:, :, cols - step :], "col", 1, col_count),
            cot_rows,
            shifted(cot_rows[:, :, :step], "col", -1, col_count),
        ],
        axis=2,
    )

    def transpose_pairs():
        pairs = []
        for a in range(row_count):
            for b in range(col_count):
                pairs.append((a * col_count + b, (b // ratio) * col_count + ratio * a + b % ratio))
        return pairs

    own_tile = lax.dynamic_slice_in_dim(right_panel, part * cols, cols + 2 * halo, 0)
    right_ext = lax.ppermute(own_tile, ("row", "col"), transpose_pairs())

    row_place = r * rows - halo + lax.broadcasted_iota(jnp.int32, (rows + 2 * halo, 1), 0)
    col_place = k * cols - halo + lax.broadcasted_iota(jnp.int32, (1, cols + 2 * halo), 1)
    valid = (row_place >= 0) & (row_place < bins) & (col_place >= 0) & (col_place < bins)
    pair_sum = left_ext.astype(jnp.float32).T[:, :, None] + right_ext.astype(jnp.float32).T[:, None, :]
    pair_ext = jnp.where(valid[None], pair_sum, 0.0).astype(jnp.bfloat16)

    ext_rows = rows + 2 * step
    ext_cols = cols + 2 * step
    conv_ext = jnp.zeros((pair_ext.shape[0], ext_rows, ext_cols), jnp.float32)
    for a in range(3):
        for b in range(3):
            conv_ext = conv_ext + depth_kernel[3 * a + b][:, None, None] * pair_ext[
                :, step * a : step * a + ext_rows, step * b : step * b + ext_cols
            ].astype(jnp.float32)
    conv_tile = conv_ext[:, step : step + rows, step : step + cols]
    hidden_state = jax.nn.silu(conv_tile).astype(jnp.bfloat16)
    mixed_out = jnp.einsum("co,cij->oij", w_point, hidden_state, preferred_element_type=jnp.float32)
    pair_tile = pair_ext[:, halo : halo + rows, halo : halo + cols]
    trunk_matrix = (pair_tile.astype(jnp.float32) + mixed_out).astype(jnp.bfloat16)

    trunk_gradient = (
        grad_scale * jnp.einsum("ch,hij->cij", w_head, cot_ext, preferred_element_type=jnp.float32)
    ).astype(jnp.bfloat16)
    grad_hidden = jnp.einsum("co,oij->cij", w_point, trunk_gradient, preferred_element_type=jnp.float32)
    conv_grad = (grad_hidden * silu_slope(conv_ext)).astype(jnp.bfloat16)
    conv_grad_tile = conv_grad[:, step : step + rows, step : step + cols].astype(jnp.float32)
    trunk_grad_tile = trunk_gradient[:, step : step + rows, step : step + cols]

    backward_pass = trunk_grad_tile.astype(jnp.float32)
    kern_terms = []
    for a in range(3):
        for b in range(3):
            backward_pass = backward_pass + depth_kernel[3 * a + b][:, None, None] * conv_grad[
                :, step * (2 - a) : step * (2 - a) + rows, step * (2 - b) : step * (2 - b) + cols
            ].astype(jnp.float32)
            window = pair_ext[
                :, step + step * a : step + step * a + rows, step + step * b : step + step * b + cols
            ].astype(jnp.float32)
            kern_terms.append(jnp.sum(conv_grad_tile * window, axis=(1, 2)))
    kernel_part = jnp.stack(kern_terms)
    left_part = jnp.sum(backward_pass, axis=2).T
    right_part = jnp.sum(backward_pass, axis=1).T
    point_part = jnp.einsum(
        "fsk,gsk->fg", hidden_state, trunk_grad_tile, preferred_element_type=jnp.float32
    )
    head_part = jnp.einsum("ydq,gdq->yg", trunk_matrix, cotangent, preferred_element_type=jnp.float32)
    small = packed((kernel_part, point_part, head_part))

    right_moved = lax.ppermute(right_part, ("row", "col"), transpose_pairs())
    bit = col_count // 2
    while bit >= ratio:
        likes = (left_part, right_moved, small)
        flat = packed(likes).astype(jnp.bfloat16)
        got = xor_round(flat, "col", col_count, bit)
        total = flat.astype(jnp.float32) + got.astype(jnp.float32)
        left_part, right_moved, small = unpacked(total, likes)
        bit //= 2
    right_block = right_moved
    bit = 1
    while bit < ratio:
        likes = (left_part, right_block, small)
        flat = packed(likes).astype(jnp.bfloat16)
        got = unpacked(xor_round(flat, "col", col_count, bit).astype(jnp.float32), likes)
        left_part, right_block, small = unpacked(flat.astype(jnp.float32), likes)
        left_part = left_part + got[0]
        small = small + got[2]
        upper = (k & bit) != 0
        right_block = jnp.concatenate(
            [jnp.where(upper, got[1], right_block), jnp.where(upper, right_block, got[1])], axis=0
        )
        bit *= 2
    grad_left = left_part.astype(jnp.bfloat16)
    grad_right = right_block.astype(jnp.bfloat16)

    grad_features = (
        jnp.dot(grad_left, w_left.T, preferred_element_type=jnp.float32)
        + jnp.dot(grad_right, w_right.T, preferred_element_type=jnp.float32)
    ).astype(jnp.bfloat16)
    contract = (((0,), (0,)), ((), ()))
    wleft_part = lax.dot_general(bin_features, grad_left, contract, preferred_element_type=jnp.float32)
    wright_part = lax.dot_general(bin_features, grad_right, contract, preferred_element_type=jnp.float32)
    wleft_part, wright_part, small = (grad_scale * wleft_part, grad_scale * wright_part, grad_scale * small)
    bit = row_count // 2
    while bit >= 1:
        likes = (wleft_part, wright_part, small)
        flat = packed(likes).astype(jnp.bfloat16)
        got = xor_round(flat, "row", row_count, bit)
        total = flat.astype(jnp.float32) + got.astype(jnp.float32)
        wleft_part, wright_part, small = unpacked(total, likes)
        bit //= 2

    kernel_sum, point_sum, head_sum = unpacked(small, (kernel_part, point_part, head_part))
    return (grad_features, wleft_part, wright_part, kernel_sum, point_sum, head_sum)


def solution(mesh):
    placed = (P("row", None), P(), P(), P(), P(), P(), P(None, "row", "col"))
    return jax.shard_map(
        body,
        mesh=mesh,
        in_specs=placed,
        out_specs=(P("row", None), P(), P(), P(), P(), P()),
        check_vma=False,
    )
```
